128 devices in a mesh: pipe: 8 (over y, x_lo), dp: 16 (over x_hi, z, core).
Axes of the slice: x: 4 (x_hi: 2, x_lo: 2; x = x_hi * 2 + x_lo), y: 4, z: 4, core: 2. Of those that a mesh axis runs over, the one named last changes fastest.
Arguments:
- clips: bfloat16 [2, 3, 2048, 1536], P(None, None, 'dp'), may hold values from -6 to 6
- positions: int32 [3, 2, 3, 2048], P(None, None, None, 'dp'), may hold values from 0 to 79, as said below
- out_proj: bfloat16 [8, 1536, 1536], P('pipe', 'dp'), may hold values from -0.15625 to 0.15625
- qk_gains: bfloat16 [8, 2, 128], P('pipe'), may hold values from -1.5 to 1.5
- cotangent: bfloat16 [2, 3, 2048, 1536], P(None, None, 'dp'), may hold values from -0.125 to 0.125
Outputs:
- grad_out_proj: float32 [8, 1536, 1536], P('pipe', 'dp')
- grad_gains: float32 [8, 2, 128], P('pipe')
The draws below stay inside these ranges and needn't reach their ends.
Inputs may be any that keep to these rules, and one draw needn't show every extreme that they name: positions[0] is a token's frame, positions[1] its row and positions[2] its column in the latent video.
All inputs are finite; a program needn't handle non-finite values.
Results may differ from the reference program's by a relative error of at most 0.018.
Values may be sent and summed in bfloat16 or wider, within the bound.
A program may use at most 192 MiB of HBM per device.

```python
import math
import jax
import jax.numpy as jnp
from jax import lax

D = 1536
HEAD = 128
TOK = 128
MICRO = 3
PHASES = 8
TOKENS = 2048


def draw_positions(key, part):
    keys = jax.random.split(key, 3)
    starts = jax.random.randint(keys[0], (2, MICRO, TOKENS // TOK, 1), 0, 30)
    within = jnp.arange(TOK, dtype=jnp.int32)
    frames = (starts + within // 64).reshape(2, MICRO, TOKENS)
    row_ids = jax.random.randint(keys[1], (2, MICRO, TOKENS), 0, 45)
    column_ids = jax.random.randint(keys[2], (2, MICRO, TOKENS), 0, 80)
    row_ids = row_ids.at[:, :, TOKENS - 1].set(0)
    column_ids = column_ids.at[:, :, TOKENS - 1].set(79)
    return jnp.stack([frames, row_ids, column_ids]).astype(jnp.int32)


def levels(stream_key, shape, cuts, low, high):
    factor_of, own = 1.0, jax.random.fold_in(stream_key, 6)
    for position, shards_of in cuts:
        heights = jnp.exp(jax.random.uniform(jax.random.fold_in(own, position), (shards_of,), jnp.float32, low / len(cuts), high / len(cuts)))
        factor_of = factor_of * jnp.repeat(heights, shape[position] // shards_of).reshape([-1 if axis == position else 1 for axis in range(len(shape))])
    return factor_of


def noise(key, dims, scale, reach, cuts=(), kind=jnp.bfloat16):
    level = levels(key, dims, cuts, -0.22, 0.18) if cuts else 1.0
    result = jax.random.normal(key, dims, jnp.float32) * scale * level
    return jnp.minimum(jnp.maximum(result, -reach), reach).astype(kind)


def setup_inputs(seed: int = 0) -> dict:
    arg_keys = jax.random.split(jax.random.key(seed), 6)
    clips = noise(arg_keys[0], (2, MICRO, TOKENS, D), 1.0, 6.0, ((2, 16),))
    positions = draw_positions(jax.random.fold_in(arg_keys[5], 71), 0)
    out_proj = noise(arg_keys[2], (PHASES, D, D), D ** -0.5, 0.15625, ((0, 8), (1, 16)))
    qk_gains = jnp.clip(jax.random.uniform(arg_keys[3], (PHASES, 2, HEAD), jnp.float32, -1.5, 1.5) * levels(arg_keys[3], (PHASES, 2, HEAD), ((0, 8),), -0.4, 0.0), -1.5, 1.5).astype(jnp.bfloat16)
    cotangent = noise(arg_keys[4], (2, MICRO, TOKENS, D), (1.0 / (2 * MICRO * TOKENS) ** 0.5), 0.125, ((2, 16),))
    return {"clips": clips, "positions": positions, "out_proj": out_proj, "qk_gains": qk_gains, "cotangent": cotangent}


def rotate(values, coords):
    head_size = values.shape[-1]
    first_width = head_size // 8
    rest_width = (head_size - first_width) // 2
    widths = (first_width, rest_width, rest_width)
    pieces = []
    offset = 0
    for axis_index in range(3):
        section = widths[axis_index]
        half_width = section // 2
        segment = values[..., offset:offset + section]
        frequency = 256.0 ** (-2.0 * jnp.arange(half_width, dtype=jnp.float32) / section)
        angles = coords[axis_index].astype(jnp.float32)[:, None] * frequency[None, :]
        cosine = jnp.cos(angles)[:, None, :]
        sine_part = jnp.sin(angles)[:, None, :]
        lower_half = segment[..., :half_width]
        upper_half = segment[..., half_width:]
        pieces.append(lower_half * cosine - upper_half * sine_part)
        pieces.append(lower_half * sine_part + upper_half * cosine)
        offset = offset + section
    return jnp.concatenate(pieces, axis=-1)

def mixing(hidden, gain_pair, coords):
    row_count, channels = hidden.shape
    head_size = gain_pair.shape[-1]
    by_heads = hidden.reshape(row_count, channels // head_size, head_size)
    wide_heads = by_heads.astype(jnp.float32)
    normed = wide_heads * lax.rsqrt(lax.optimization_barrier(jnp.mean(wide_heads * wide_heads, axis=-1, keepdims=True)) + 1e-06)
    queries = rotate(normed * gain_pair[0], coords)
    key_rows = rotate(normed * gain_pair[1], coords)
    scores = jnp.einsum('qhe,khe->hqk', queries, key_rows, precision=lax.Precision.HIGHEST) / math.sqrt(head_size)
    exp_scores = jnp.exp(scores)
    weights = (exp_scores / lax.optimization_barrier(jnp.sum(exp_scores, axis=-1, keepdims=True))).astype(jnp.bfloat16)
    weights_wide = lax.optimization_barrier(weights).astype(jnp.float32)
    mixed_rows = jnp.einsum('hqk,khe->qhe', weights_wide, wide_heads)
    return mixed_rows.reshape(row_count, channels).astype(jnp.bfloat16)

def phase_forward(hidden, gain_pair, coords, weight):
    mixed_rows = mixing(hidden, gain_pair, coords)
    update = jnp.dot(mixed_rows, weight, preferred_element_type=jnp.float32)
    return (hidden.astype(jnp.float32) + update).astype(jnp.bfloat16)

def phase_backward(hidden, gain_pair, coords, weight, grad_out):

    def local_mix(state_rows, gain_values):
        return mixing(state_rows, gain_values, coords)
    mixed_rows, pullback = jax.vjp(local_mix, hidden, gain_pair)
    weight_term = lax.dot_general(mixed_rows, grad_out, (((0,), (0,)), ((), ())), preferred_element_type=jnp.float32)
    grad_mixed = lax.dot_general(grad_out, weight, (((1,), (1,)), ((), ())), preferred_element_type=jnp.float32).astype(jnp.bfloat16)
    grad_hidden, gain_term = pullback(grad_mixed)
    grad_in = (grad_out.astype(jnp.float32) + grad_hidden.astype(jnp.float32)).astype(jnp.bfloat16)
    return (grad_in, weight_term, gain_term)

def reference(clips, positions, out_proj, qk_gains, cotangent):
    phase_count = out_proj.shape[0]
    micro_count = clips.shape[1]
    channels = clips.shape[3]
    group_count = clips.shape[2] // TOK
    batch_count = 2 * micro_count * group_count
    all_rows = clips.reshape(batch_count, TOK, channels)
    coord_rows = jnp.transpose(positions.reshape(3, batch_count, TOK), (1, 0, 2))
    cot_rows = cotangent.reshape(batch_count, TOK, channels)
    gain_table = qk_gains.astype(jnp.float32)
    forward_map = jax.vmap(phase_forward, in_axes=(0, None, 0, None))
    inputs = []
    hidden = all_rows
    for phase_index in range(phase_count):
        inputs.append(hidden)
        hidden = forward_map(hidden, gain_table[phase_index], coord_rows, out_proj[phase_index])
    grad_rows = cot_rows
    weight_grads = [None] * phase_count
    gain_grads = [None] * phase_count
    for phase_index in reversed(range(phase_count)):
        gain_pair = gain_table[phase_index]
        weight = out_proj[phase_index]

        def backward_one(carry, batch_item):
            state_rows, coord_item, grad_item = batch_item
            grad_in, weight_term, gain_term = phase_backward(state_rows, gain_pair, coord_item, weight, grad_item)
            return ((carry[0] + weight_term, carry[1] + gain_term), grad_in)
        start_sums = (jnp.zeros((channels, channels), jnp.float32), jnp.zeros(gain_pair.shape, jnp.float32))
        totals, grad_rows = lax.scan(backward_one, start_sums, (inputs[phase_index], coord_rows, grad_rows))
        weight_grads[phase_index] = totals[0]
        gain_grads[phase_index] = totals[1]
    return (jnp.stack(weight_grads), jnp.stack(gain_grads))
```

```python
import functools
import math

import jax
import jax.numpy as jnp
import numpy as np
from jax import lax
from jax.experimental import pallas as pl
from jax.experimental.pallas import tpu as pltpu
from jax.sharding import PartitionSpec as P

D = 1536
HEAD = 128
TOK = 128
HEADS = D // HEAD
PHASES = 8
F32 = jnp.float32
BF16 = jnp.bfloat16

NN = (((1,), (0,)), ((), ()))
NT = (((1,), (1,)), ((), ()))
TN = (((0,), (0,)), ((), ()))


def dot(a, b, dims=NN, precision=None):
    return lax.dot_general(a, b, dims, precision=precision, preferred_element_type=F32)


def rotary_constants():
    first = HEAD // 8
    rest = (HEAD - first) // 2
    freq = np.zeros((8, HEAD), np.float32)
    partner = np.zeros(HEAD, np.int32)
    sign = np.zeros((1, HEAD), np.float32)
    offset = 0
    for axis, width in enumerate((first, rest, rest)):
        half = width // 2
        values = np.float32(256.0) ** (np.float32(-2.0) * np.arange(half, dtype=np.float32) / np.float32(width))
        low = np.arange(offset, offset + half)
        high = low + half
        freq[axis, low] = values
        freq[axis, high] = values
        partner[low], partner[high] = high, low
        sign[0, low], sign[0, high] = -1.0, 1.0
        offset += width
    swap = np.zeros((HEAD, HEAD), np.float32)
    swap[partner, np.arange(HEAD)] = 1.0
    return freq, swap, sign


def head(j):
    return pl.ds(j * HEAD, HEAD)


def forward_phase(s, w_ref, tabs, swap, hs, qs, ks, es, ms, ns, rcols, icols):
    a0, b0, a1, b1 = tabs
    ones = jnp.ones((TOK, HEAD), BF16)
    for j in range(HEADS):
        hj = hs[s, :, head(j)]
        hf = hj.astype(F32)
        r = lax.rsqrt(jnp.mean(hf * hf, axis=-1, keepdims=True) + 1e-6)
        rcols[s, :, j : j + 1] = r
        n = hf * r
        nsw = dot(hj, swap) * r
        ns[s, :, head(j)] = nsw.astype(BF16)
        qs[s, :, head(j)] = (n * a0 + nsw * b0).astype(BF16)
        ks[s, :, head(j)] = (n * a1 + nsw * b1).astype(BF16)
    for j in range(HEADS):
        scores = dot(qs[s, :, head(j)], ks[s, :, head(j)], NT)
        es[s, :, head(j)] = jnp.exp(scores).astype(BF16)
    for j in range(HEADS):
        both = dot(es[s, :, head(j)], jnp.concatenate([hs[s, :, head(j)], ones], axis=1))
        inv = 1.0 / both[:, HEAD:]
        icols[s, :, j : j + 1] = inv[:, 0:1]
        ms[s, :, head(j)] = (both[:, :HEAD] * inv).astype(BF16)
    for c in range(D // 512):
        cols = pl.ds(c * 512, 512)
        update = dot(ms[s], w_ref[0, :, cols])
        hs[s + 1, :, cols] = (hs[s, :, cols].astype(F32) + update).astype(BF16)


def backward_phase(s, w_ref, tabs, swap, g, gm, acc, hs, qs, ks, es, ms, ns, rcols, icols, grad_ref):
    a0, b0, a1, b1 = tabs
    for c in range(D // 512):
        cols = pl.ds(c * 512, 512)
        gm[:, cols] = dot(g[...], w_ref[0, cols, :], NT).astype(BF16)
    for c in range(D // 512):
        cols = pl.ds(c * 512, 512)
        for t in range(D // 512):
            rows = pl.ds(t * 512, 512)
            grad_ref[0, rows, cols] = dot(ms[s, :, rows], g[:, cols], TN).astype(BF16)
    acc[...] = jnp.zeros_like(acc)
    for j in range(HEADS):
        hj = hs[s, :, head(j)]
        ej = es[s, :, head(j)]
        qj = qs[s, :, head(j)]
        kj = ks[s, :, head(j)]
        r = rcols[s, :, j : j + 1]
        gmf = gm[:, head(j)].astype(F32) * icols[s, :, j : j + 1]
        delta = jnp.sum(gmf * ms[s, :, head(j)].astype(F32), axis=-1, keepdims=True)
        gmb = gmf.astype(BF16)
        ga = dot(gmb, hj, NT)
        ds = (ej.astype(F32) * (ga - delta)).astype(BF16)
        gv = dot(ej, gmb, TN)
        dq = dot(ds, kj)
        dk = dot(ds, qj, TN)
        n = hj.astype(F32) * r
        nsw = ns[s, :, head(j)].astype(F32)
        acc[0] += n * dq
        acc[1] += nsw * dq
        acc[2] += n * dk
        acc[3] += nsw * dk
        crossed = (dq * b0 + dk * b1).astype(BF16)
        dn = dq * a0 + dk * a1 + dot(crossed, swap, NT)
        dh = r * (dn - n * jnp.mean(dn * n, axis=-1, keepdims=True))
        g[:, head(j)] = (g[:, head(j)].astype(F32) + (dh + gv)).astype(BF16)


def compute_kernel(place_ref, clip_ref, pos_ref, cot_ref, gains_ref, swapped_ref, freq_ref, swap_ref, sign_ref, w_ref,
                   grad_ref, dgain_ref, hs, qs, ks, es, ms, ns, rcols, icols, g, gm, acc, cosine, sine):
    step = pl.program_id(0)
    live = place_ref[0] < 6
    scale = 1.0 / math.sqrt(HEAD)
    swap = swap_ref[...]

    def tables(s):
        ga = gains_ref[s].astype(F32)
        gs = swapped_ref[s].astype(F32)
        c, n = cosine[...], sine[...]
        return (c * (ga[0:1] * scale), n * (gs[0:1] * scale), c * ga[1:2], n * gs[1:2])

    saved = (hs, qs, ks, es, ms, ns, rcols, icols)

    @pl.when(live & (step == 0))
    def _():
        p = place_ref[0]
        positions = pos_ref[:, p // 3, p % 3, :].astype(F32)
        padded = jnp.concatenate([positions, jnp.zeros((5, TOK), F32)], axis=0)
        angles = dot(padded, freq_ref[...], TN, lax.Precision.HIGHEST)
        cosine[...] = jnp.cos(angles)
        sine[...] = jnp.sin(angles) * sign_ref[...]
        hs[0] = clip_ref[0, 0]

    @pl.when(live & (step < PHASES))
    def _():
        forward_phase(step, w_ref, tables(step), swap, *saved)

    @pl.when(live & (step == PHASES))
    def _():
        g[...] = cot_ref[0, 0]

    @pl.when(live & (step >= PHASES))
    def _():
        s = 2 * PHASES - 1 - step
        backward_phase(s, w_ref, tables(s), swap, g, gm, acc, *saved, grad_ref)
        x0 = jnp.sum(acc[0] * cosine[...], axis=0, keepdims=True)
        y0 = jnp.sum(acc[1] * sine[...], axis=0, keepdims=True)
        x1 = jnp.sum(acc[2] * cosine[...], axis=0, keepdims=True)
        y1 = jnp.sum(acc[3] * sine[...], axis=0, keepdims=True)
        rows = jnp.concatenate([x0 * scale, x1, y0 * scale, y1, jnp.zeros((4, HEAD), F32)], axis=0)
        dgain_ref[0] = rows

    @pl.when(jnp.logical_not(live) & (step >= PHASES))
    def _():
        grad_ref[...] = jnp.zeros_like(grad_ref)
        dgain_ref[...] = jnp.zeros_like(dgain_ref)


def compute(place, clips, positions, cotangent, gains, swapped, weights):
    freq, swap, sign = rotary_constants()

    def group(i, place_ref):
        p = jnp.minimum(place_ref[0], 5)
        return (p // 3, p % 3)

    def phase_of(i):
        return jnp.minimum(i, 2 * PHASES - 1 - i)

    def out_phase(i):
        return jnp.minimum(2 * PHASES - 1 - i, PHASES - 1)

    whole = lambda rank: (lambda i, p: (0,) * rank)
    spec = pltpu.PrefetchScalarGridSpec(
        num_scalar_prefetch=1,
        grid=(2 * PHASES,),
        in_specs=[
            pl.BlockSpec((1, 1, TOK, D), lambda i, p: (*group(i, p), 0, 0)),
            pl.BlockSpec((3, 2, 3, TOK), whole(4)),
            pl.BlockSpec((1, 1, TOK, D), lambda i, p: (*group(i, p), 0, 0)),
            pl.BlockSpec((PHASES, 2, HEAD), whole(3)),
            pl.BlockSpec((PHASES, 2, HEAD), whole(3)),
            pl.BlockSpec((8, HEAD), whole(2)),
            pl.BlockSpec((HEAD, HEAD), whole(2)),
            pl.BlockSpec((1, HEAD), whole(2)),
            pl.BlockSpec((1, D, D), lambda i, p: (phase_of(i), 0, 0)),
        ],
        out_specs=[
            pl.BlockSpec((1, D, D), lambda i, p: (out_phase(i), 0, 0)),
            pl.BlockSpec((1, 8, HEAD), lambda i, p: (out_phase(i), 0, 0)),
        ],
        scratch_shapes=[
            pltpu.VMEM((PHASES + 1, TOK, D), BF16),
            pltpu.VMEM((PHASES, TOK, D), BF16),
            pltpu.VMEM((PHASES, TOK, D), BF16),
            pltpu.VMEM((PHASES, TOK, D), BF16),
            pltpu.VMEM((PHASES, TOK, D), BF16),
            pltpu.VMEM((PHASES, TOK, D), BF16),
            pltpu.VMEM((PHASES, TOK, HEAD), F32),
            pltpu.VMEM((PHASES, TOK, HEAD), F32),
            pltpu.VMEM((TOK, D), BF16),
            pltpu.VMEM((TOK, D), BF16),
            pltpu.VMEM((4, TOK, HEAD), F32),
            pltpu.VMEM((TOK, HEAD), F32),
            pltpu.VMEM((TOK, HEAD), F32),
        ],
    )
    return pl.pallas_call(
        compute_kernel,
        grid_spec=spec,
        out_shape=(
            jax.ShapeDtypeStruct((PHASES, D, D), BF16),
            jax.ShapeDtypeStruct((PHASES, 8, HEAD), F32),
        ),
        compiler_params=pltpu.CompilerParams(
            dimension_semantics=("arbitrary",), vmem_limit_bytes=60 << 20
        ),
        name="phases",
    )(
        place, clips, positions, cotangent, gains, swapped, jnp.asarray(freq),
        jnp.asarray(swap, BF16), jnp.asarray(sign), weights,
    )


def shards(clips, positions, out_proj, qk_gains, cotangent):
    place = lax.axis_index("pipe")
    _, swap, _ = rotary_constants()
    partner = np.argmax(swap, axis=0)
    weights = lax.all_gather(out_proj[0], ("pipe", "dp"), axis=0, tiled=True).reshape(PHASES, D, D)
    gains = lax.all_gather(qk_gains[0], "pipe", axis=0)
    swapped = gains[:, :, partner]
    grads, dgains = compute(place[None], clips, positions, cotangent, gains, swapped, weights)
    shard = lax.psum_scatter(
        grads.reshape(PHASES * D, D), ("pipe", "dp"), scatter_dimension=0, tiled=True
    )
    total = lax.psum(dgains, ("pipe", "dp"))
    mine = lax.dynamic_index_in_dim(total, place, 0, keepdims=True)
    dgain = mine[:, 0:2] + mine[:, 2:4][:, :, partner]
    return (shard.astype(F32)[None], dgain)


def solution(mesh):
    placed = (
        P(None, None, "dp", None),
        P(None, None, None, "dp"),
        P("pipe", "dp", None),
        P("pipe", None, None),
        P(None, None, "dp", None),
    )
    return jax.shard_map(
        shards,
        mesh=mesh,
        in_specs=placed,
        out_specs=(P("pipe", "dp", None), P("pipe", None, None)),
        check_vma=False,
    )
```

```python
import functools
import math

import jax
import jax.numpy as jnp
import numpy as np
from jax import lax
from jax.experimental import pallas as pl
from jax.experimental.pallas import tpu as pltpu
from jax.sharding import PartitionSpec as P

D = 1536
HEAD = 128
TOK = 128
HEADS = D // HEAD
PHASES = 8
F32 = jnp.float32
BF16 = jnp.bfloat16

NN = (((1,), (0,)), ((), ()))
NT = (((1,), (1,)), ((), ()))
TN = (((0,), (0,)), ((), ()))


def dot(a, b, dims=NN, precision=None):
    return lax.dot_general(a, b, dims, precision=precision, preferred_element_type=F32)


def rotary_constants():
    first = HEAD // 8
    rest = (HEAD - first) // 2
    freq = np.zeros((8, HEAD), np.float32)
    partner = np.zeros(HEAD, np.int32)
    sign = np.zeros((1, HEAD), np.float32)
    offset = 0
    for axis, width in enumerate((first, rest, rest)):
        half = width // 2
        values = np.float32(256.0) ** (np.float32(-2.0) * np.arange(half, dtype=np.float32) / np.float32(width))
        low = np.arange(offset, offset + half)
        high = low + half
        freq[axis, low] = values
        freq[axis, high] = values
        partner[low], partner[high] = high, low
        sign[0, low], sign[0, high] = -1.0, 1.0
        offset += width
    swap = np.zeros((HEAD, HEAD), np.float32)
    swap[partner, np.arange(HEAD)] = 1.0
    return freq, swap, sign


MESH = pl.DeviceIdType.MESH
AXES = "xyz"
ORDERS = ("xyz", "yzx", "zxy")


class Place:
    def __init__(self):
        self.pipe = lax.axis_index("pipe")
        self.dp = lax.axis_index("dp")
        self.core = self.dp % 2
        self.at = {
            "x": self.dp // 8 * 2 + self.pipe % 2,
            "y": self.pipe // 2,
            "z": self.dp // 2 % 4,
        }

    def device(self, core=None, **moved):
        c = {**self.at, **moved}
        core = self.core if core is None else core
        return (c["y"] * 2 + c["x"] % 2, (c["x"] // 2 * 4 + c["z"]) * 2 + core)

    def step(self, axis, delta):
        return (self.at[axis] + delta + 4) % 4

    def neighbour(self, axis, delta):
        return self.device(**{axis: self.step(axis, delta)})

    def sibling(self):
        return self.device(core=1 - self.core)


def greet(place):
    barrier = pltpu.get_barrier_semaphore()
    others = [place.neighbour(axis, delta) for axis in AXES for delta in (1, -1, 2)]
    others.append(place.sibling())
    others += [((place.pipe + q) % PHASES, place.dp) for q in range(1, PHASES)]
    for other in others:
        pl.semaphore_signal(barrier, inc=1, device_id=other, device_id_type=MESH)
    pl.semaphore_wait(barrier, len(others))


WHOLE = "whole"


def half(h):
    return ("half", h)


def block(ref, lead, k, core, x, y, z):
    def plain(v):
        if v is WHOLE:
            return slice(None)
        return pl.ds(2 * v[1], 2) if isinstance(v, tuple) else v

    if x is WHOLE:
        xh, xl = slice(None), slice(None)
    elif isinstance(x, tuple):
        xh, xl = x[1], slice(None)
    else:
        xh, xl = x // 2, x % 2
    return ref.at[(*lead, plain(y), xh, plain(z), core, xl, k)]


TILES = (4, 2, 4, 2, 2, 3, 16, D // 4)


def gather_kernel(shard_ref, gain_ref, w_ref, gains_ref, first_send, first_recv, gain_send, gain_recv, local_sem, send, recv):
    place = Place()
    greet(place)
    me = place.pipe
    mine = dict(place.at)

    def first(q, owner, target):
        return pltpu.make_async_remote_copy(
            src_ref=shard_ref.at[0, q % 2, :, :, pl.ds(pl.multiple_of(q // 2 * (D // 4), 128), D // 4)],
            dst_ref=w_ref.at[owner, q // 2, place.dp // 8, place.dp // 2 % 4, place.core, q % 2],
            send_sem=first_send.at[q],
            recv_sem=first_recv.at[owner],
            device_id=(target, place.dp),
            device_id_type=MESH,
        )

    def gain(owner, q):
        return pltpu.make_async_remote_copy(
            src_ref=gain_ref.at[0],
            dst_ref=gains_ref.at[owner],
            send_sem=gain_send.at[q],
            recv_sem=gain_recv.at[owner],
            device_id=(q, place.dp),
            device_id_type=MESH,
        )

    own = pltpu.make_async_copy(
        shard_ref.at[0, me % 2, :, :, pl.ds(pl.multiple_of(me // 2 * (D // 4), 128), D // 4)],
        w_ref.at[me, me // 2, place.dp // 8, place.dp // 2 % 4, place.core, me % 2],
        local_sem.at[0],
    )
    own_gain = pltpu.make_async_copy(gain_ref.at[0], gains_ref.at[me], local_sem.at[1])
    own.start()
    own_gain.start()
    for q in range(PHASES):
        @pl.when(q != me)
        def _():
            first(q, me, q).start()
            gain(me, q).start()
    for q in range(PHASES):
        @pl.when(q != me)
        def _():
            first(q, me, q).wait_send()
            gain(me, q).wait_send()
            first(q, q, q).wait_recv()
            gain(q, q).wait_recv()
    own.wait()
    own_gain.wait()

    def copies(stage, s, parity):
        made = []

        def add(view, device):
            i = stage_base[stage] + len(made)
            made.append(pltpu.make_async_remote_copy(
                src_ref=view,
                dst_ref=view,
                send_sem=send.at[parity, i],
                recv_sem=recv.at[parity, i],
                device_id=device,
                device_id_type=MESH,
            ))

        if stage == 5:
            add(w_ref.at[s, :, :, :, place.core], place.sibling())
            return made
        for k, (a, b, c) in enumerate(ORDERS):
            def view(**where):
                return block(w_ref, (s,), k, place.core, **{**mine, **where})

            if stage == 0:
                for delta in (1, -1, 2):
                    add(view(), place.neighbour(c, delta))
            elif stage == 1:
                for delta in (1, -1):
                    add(view(**{c: WHOLE}), place.neighbour(b, delta))
            elif stage == 2:
                for h, delta in enumerate((1, -1)):
                    add(view(**{b: place.step(b, -delta), c: half(h)}), place.neighbour(b, delta))
            elif stage == 3:
                for delta in (1, -1):
                    add(view(**{b: WHOLE, c: WHOLE}), place.neighbour(a, delta))
            else:
                for h, delta in enumerate((1, -1)):
                    add(view(**{a: place.step(a, -delta), b: half(h), c: WHOLE}), place.neighbour(a, delta))
        return made

    stage_base = (0, 9, 15, 21, 27, 33)

    def tick(t, carry):
        for stage in range(6):
            s = t - 1 - stage

            @pl.when((s >= 0) & (s < PHASES))
            def _():
                for copy in copies(stage, s, (t + 1) % 2):
                    copy.wait()
        for stage in range(6):
            s = t - stage

            @pl.when((s >= 0) & (s < PHASES))
            def _():
                for copy in copies(stage, s, t % 2):
                    copy.start()
        return carry

    lax.fori_loop(0, PHASES + 6, tick, 0)


def gather(shard, gain_rows):
    anywhere = pl.BlockSpec(memory_space=pl.ANY)
    return pl.pallas_call(
        gather_kernel,
        out_shape=(
            jax.ShapeDtypeStruct((PHASES, *TILES), BF16),
            jax.ShapeDtypeStruct((PHASES, 8, HEAD), F32),
        ),
        in_specs=[anywhere, anywhere],
        out_specs=[anywhere, anywhere],
        scratch_shapes=[
            pltpu.SemaphoreType.DMA((PHASES,)),
            pltpu.SemaphoreType.DMA((PHASES,)),
            pltpu.SemaphoreType.DMA((PHASES,)),
            pltpu.SemaphoreType.DMA((PHASES,)),
            pltpu.SemaphoreType.DMA((2,)),
            pltpu.SemaphoreType.DMA((2, 34)),
            pltpu.SemaphoreType.DMA((2, 34)),
        ],
        compiler_params=pltpu.CompilerParams(collective_id=0, has_side_effects=True),
        name="gather",
    )(shard, gain_rows)


def head(j):
    return pl.ds(j * HEAD, HEAD)


def forward_phase(s, w_ref, tabs, swap, hs, qs, ks, es, ms, ns, rcols, icols):
    a0, b0, a1, b1 = tabs
    ones = jnp.ones((TOK, HEAD), BF16)
    for j in range(HEADS):
        hj = hs[s, :, head(j)]
        hf = hj.astype(F32)
        r = lax.rsqrt(jnp.mean(hf * hf, axis=-1, keepdims=True) + 1e-6)
        rcols[s, :, j : j + 1] = r
        n = hf * r
        nsw = dot(hj, swap) * r
        ns[s, :, head(j)] = nsw.astype(BF16)
        qs[s, :, head(j)] = (n * a0 + nsw * b0).astype(BF16)
        ks[s, :, head(j)] = (n * a1 + nsw * b1).astype(BF16)
    for j in range(HEADS):
        scores = dot(qs[s, :, head(j)], ks[s, :, head(j)], NT)
        es[s, :, head(j)] = jnp.exp(scores).astype(BF16)
    for j in range(HEADS):
        both = dot(es[s, :, head(j)], jnp.concatenate([hs[s, :, head(j)], ones], axis=1))
        inv = 1.0 / both[:, HEAD:]
        icols[s, :, j : j + 1] = inv[:, 0:1]
        ms[s, :, head(j)] = (both[:, :HEAD] * inv).astype(BF16)
    for c in range(4):
        cols = pl.ds(c * 384, 384)
        update = dot(ms[s], w_ref[0, c])
        hs[s + 1, :, cols] = (hs[s, :, cols].astype(F32) + update).astype(BF16)


def backward_phase(s, w_ref, tabs, swap, g, gm, acc, hs, qs, ks, es, ms, ns, rcols, icols, grad_ref):
    a0, b0, a1, b1 = tabs
    for c in range(D // 512):
        cols = pl.ds(c * 512, 512)
        total = dot(g[:, 0:384], w_ref[0, 0, cols, :], NT)
        for y in range(1, 4):
            total += dot(g[:, pl.ds(y * 384, 384)], w_ref[0, y, cols, :], NT)
        gm[:, cols] = total.astype(BF16)
    for c in range(D // 512):
        cols = pl.ds(c * 512, 512)
        for t in range(D // 512):
            rows = pl.ds(t * 512, 512)
            grad_ref[0, rows, cols] = dot(ms[s, :, rows], g[:, cols], TN).astype(BF16)
    acc[...] = jnp.zeros_like(acc)
    for j in range(HEADS):
        hj = hs[s, :, head(j)]
        ej = es[s, :, head(j)]
        qj = qs[s, :, head(j)]
        kj = ks[s, :, head(j)]
        r = rcols[s, :, j : j + 1]
        gmf = gm[:, head(j)].astype(F32) * icols[s, :, j : j + 1]
        delta = jnp.sum(gmf * ms[s, :, head(j)].astype(F32), axis=-1, keepdims=True)
        gmb = gmf.astype(BF16)
        ga = dot(gmb, hj, NT)
        ds = (ej.astype(F32) * (ga - delta)).astype(BF16)
        gv = dot(ej, gmb, TN)
        dq = dot(ds, kj)
        dk = dot(ds, qj, TN)
        n = hj.astype(F32) * r
        nsw = ns[s, :, head(j)].astype(F32)
        acc[0] += n * dq
        acc[1] += nsw * dq
        acc[2] += n * dk
        acc[3] += nsw * dk
        crossed = (dq * b0 + dk * b1).astype(BF16)
        dn = dq * a0 + dk * a1 + dot(crossed, swap, NT)
        dh = r * (dn - n * jnp.mean(dn * n, axis=-1, keepdims=True))
        g[:, head(j)] = (g[:, head(j)].astype(F32) + (dh + gv)).astype(BF16)


def compute_kernel(place_ref, clip_ref, pos_ref, cot_ref, gains_ref, freq_ref, swap_ref, sign_ref, w_ref,
                   grad_ref, dgain_ref, hs, qs, ks, es, ms, ns, rcols, icols, g, gm, acc, cosine, sine):
    step = pl.program_id(0)
    live = place_ref[0] < 6
    scale = 1.0 / math.sqrt(HEAD)
    swap = swap_ref[...]

    def tables(s):
        rows = gains_ref[s]
        c, n = cosine[...], sine[...]
        return (c * (rows[0:1] * scale), n * (rows[2:3] * scale), c * rows[1:2], n * rows[3:4])

    saved = (hs, qs, ks, es, ms, ns, rcols, icols)

    @pl.when(live & (step == 0))
    def _():
        p = place_ref[0]
        positions = pos_ref[:, p // 3, p % 3, :].astype(F32)
        padded = jnp.concatenate([positions, jnp.zeros((5, TOK), F32)], axis=0)
        angles = dot(padded, freq_ref[...], TN, lax.Precision.HIGHEST)
        cosine[...] = jnp.cos(angles)
        sine[...] = jnp.sin(angles) * sign_ref[...]
        hs[0] = clip_ref[0, 0]

    @pl.when(live & (step < PHASES))
    def _():
        forward_phase(step, w_ref, tables(step), swap, *saved)

    @pl.when(live & (step == PHASES))
    def _():
        g[...] = cot_ref[0, 0]

    @pl.when(live & (step >= PHASES))
    def _():
        s = 2 * PHASES - 1 - step
        backward_phase(s, w_ref, tables(s), swap, g, gm, acc, *saved, grad_ref)
        x0 = jnp.sum(acc[0] * cosine[...], axis=0, keepdims=True)
        y0 = jnp.sum(acc[1] * sine[...], axis=0, keepdims=True)
        x1 = jnp.sum(acc[2] * cosine[...], axis=0, keepdims=True)
        y1 = jnp.sum(acc[3] * sine[...], axis=0, keepdims=True)
        rows = jnp.concatenate([x0 * scale, x1, y0 * scale, y1, jnp.zeros((4, HEAD), F32)], axis=0)
        dgain_ref[0] = rows

    @pl.when(jnp.logical_not(live) & (step >= PHASES))
    def _():
        grad_ref[...] = jnp.zeros_like(grad_ref)
        dgain_ref[...] = jnp.zeros_like(dgain_ref)


def compute(place, clips, positions, cotangent, gains, weights):
    freq, swap, sign = rotary_constants()

    def group(i, place_ref):
        p = jnp.minimum(place_ref[0], 5)
        return (p // 3, p % 3)

    def phase_of(i):
        return jnp.minimum(i, 2 * PHASES - 1 - i)

    def out_phase(i):
        return jnp.minimum(2 * PHASES - 1 - i, PHASES - 1)

    whole = lambda rank: (lambda i, p: (0,) * rank)
    spec = pltpu.PrefetchScalarGridSpec(
        num_scalar_prefetch=1,
        grid=(2 * PHASES,),
        in_specs=[
            pl.BlockSpec((1, 1, TOK, D), lambda i, p: (*group(i, p), 0, 0)),
            pl.BlockSpec((3, 2, 3, TOK), whole(4)),
            pl.BlockSpec((1, 1, TOK, D), lambda i, p: (*group(i, p), 0, 0)),
            pl.BlockSpec((PHASES, 8, HEAD), whole(3)),
            pl.BlockSpec((8, HEAD), whole(2)),
            pl.BlockSpec((HEAD, HEAD), whole(2)),
            pl.BlockSpec((1, HEAD), whole(2)),
            pl.BlockSpec((1, 4, D, D // 4), lambda i, p: (phase_of(i), 0, 0, 0)),
        ],
        out_specs=[
            pl.BlockSpec((1, D, D), lambda i, p: (out_phase(i), 0, 0)),
            pl.BlockSpec((1, 8, HEAD), lambda i, p: (out_phase(i), 0, 0)),
        ],
        scratch_shapes=[
            pltpu.VMEM((PHASES + 1, TOK, D), BF16),
            pltpu.VMEM((PHASES, TOK, D), BF16),
            pltpu.VMEM((PHASES, TOK, D), BF16),
            pltpu.VMEM((PHASES, TOK, D), BF16),
            pltpu.VMEM((PHASES, TOK, D), BF16),
            pltpu.VMEM((PHASES, TOK, D), BF16),
            pltpu.VMEM((PHASES, TOK, HEAD), F32),
            pltpu.VMEM((PHASES, TOK, HEAD), F32),
            pltpu.VMEM((TOK, D), BF16),
            pltpu.VMEM((TOK, D), BF16),
            pltpu.VMEM((4, TOK, HEAD), F32),
            pltpu.VMEM((TOK, HEAD), F32),
            pltpu.VMEM((TOK, HEAD), F32),
        ],
    )
    return pl.pallas_call(
        compute_kernel,
        grid_spec=spec,
        out_shape=(
            jax.ShapeDtypeStruct((PHASES, D, D), BF16),
            jax.ShapeDtypeStruct((PHASES, 8, HEAD), F32),
        ),
        compiler_params=pltpu.CompilerParams(
            dimension_semantics=("arbitrary",), vmem_limit_bytes=60 << 20
        ),
        name="phases",
    )(
        place, clips, positions, cotangent, gains, jnp.asarray(freq),
        jnp.asarray(swap, BF16), jnp.asarray(sign), weights,
    )


def shards(clips, positions, out_proj, qk_gains, cotangent):
    place = lax.axis_index("pipe")
    _, swap, _ = rotary_constants()
    partner = np.argmax(swap, axis=0)
    own = qk_gains[0].astype(F32)
    gain_rows = jnp.concatenate([own, own[:, partner], jnp.zeros((4, HEAD), F32)], axis=0)[None]
    tiles, gains = gather(out_proj.reshape(1, 2, 3, 16, D), gain_rows)
    weights = tiles.reshape(PHASES, 4, D, D // 4)
    grads, dgains = compute(place[None], clips, positions, cotangent, gains, weights)
    shard = lax.psum_scatter(
        grads.reshape(PHASES * D, D), ("pipe", "dp"), scatter_dimension=0, tiled=True
    )
    total = lax.psum(dgains, ("pipe", "dp"))
    mine = lax.dynamic_index_in_dim(total, place, 0, keepdims=True)
    dgain = mine[:, 0:2] + mine[:, 2:4][:, :, partner]
    return (shard.astype(F32)[None], dgain)


def solution(mesh):
    placed = (
        P(None, None, "dp", None),
        P(None, None, None, "dp"),
        P("pipe", "dp", None),
        P("pipe", None, None),
        P(None, None, "dp", None),
    )
    return jax.shard_map(
        shards,
        mesh=mesh,
        in_specs=placed,
        out_specs=(P("pipe", "dp", None), P("pipe", None, None)),
        check_vma=False,
    )
```

```python
import functools
import math

import jax
import jax.numpy as jnp
import numpy as np
from jax import lax
from jax.experimental import pallas as pl
from jax.experimental.pallas import tpu as pltpu
from jax.sharding import PartitionSpec as P

D = 1536
HEAD = 128
TOK = 128
HEADS = D // HEAD
PHASES = 8
F32 = jnp.float32
BF16 = jnp.bfloat16

NN = (((1,), (0,)), ((), ()))
NT = (((1,), (1,)), ((), ()))
TN = (((0,), (0,)), ((), ()))


def dot(a, b, dims=NN, precision=None):
    return lax.dot_general(a, b, dims, precision=precision, preferred_element_type=F32)


def rotary_constants():
    first = HEAD // 8
    rest = (HEAD - first) // 2
    freq = np.zeros((8, HEAD), np.float32)
    partner = np.zeros(HEAD, np.int32)
    sign = np.zeros((1, HEAD), np.float32)
    offset = 0
    for axis, width in enumerate((first, rest, rest)):
        half = width // 2
        values = np.float32(256.0) ** (np.float32(-2.0) * np.arange(half, dtype=np.float32) / np.float32(width))
        low = np.arange(offset, offset + half)
        high = low + half
        freq[axis, low] = values
        freq[axis, high] = values
        partner[low], partner[high] = high, low
        sign[0, low], sign[0, high] = -1.0, 1.0
        offset += width
    swap = np.zeros((HEAD, HEAD), np.float32)
    swap[partner, np.arange(HEAD)] = 1.0
    return freq, swap, sign


MESH = pl.DeviceIdType.MESH
AXES = "xyz"
ORDERS = ("xyz", "yzx", "zxy")


class Place:
    def __init__(self):
        self.pipe = lax.axis_index("pipe")
        self.dp = lax.axis_index("dp")
        self.core = self.dp % 2
        self.at = {
            "x": self.dp // 8 * 2 + self.pipe % 2,
            "y": self.pipe // 2,
            "z": self.dp // 2 % 4,
        }

    def device(self, core=None, **moved):
        c = {**self.at, **moved}
        core = self.core if core is None else core
        return (c["y"] * 2 + c["x"] % 2, (c["x"] // 2 * 4 + c["z"]) * 2 + core)

    def step(self, axis, delta):
        return (self.at[axis] + delta + 4) % 4

    def neighbour(self, axis, delta):
        return self.device(**{axis: self.step(axis, delta)})

    def sibling(self):
        return self.device(core=1 - self.core)


def greet(place, wide=False):
    barrier = pltpu.get_barrier_semaphore()
    others = [place.neighbour(axis, delta) for axis in AXES for delta in (1, -1, 2)]
    others.append(place.sibling())
    others += [((place.pipe + q) % PHASES, place.dp) for q in range(1, PHASES)]
    if wide:
        others += [(place.pipe, (place.dp + q) % WIDE_PEERS) for q in range(1, WIDE_PEERS)]
    for other in others:
        pl.semaphore_signal(barrier, inc=1, device_id=other, device_id_type=MESH)
    pl.semaphore_wait(barrier, len(others))


WHOLE = "whole"


def half(h):
    return ("half", h)


def block(ref, lead, k, core, x, y, z):
    def plain(v):
        if v is WHOLE:
            return slice(None)
        return pl.ds(2 * v[1], 2) if isinstance(v, tuple) else v

    if x is WHOLE:
        xh, xl = slice(None), slice(None)
    elif isinstance(x, tuple):
        xh, xl = x[1], slice(None)
    else:
        xh, xl = x // 2, x % 2
    return ref.at[(*lead, plain(y), xh, plain(z), core, xl, k)]


TILES = (4, 2, 4, 2, 2, 3, 16, D // 4)


def gather_kernel(shard_ref, gain_ref, w_ref, gains_ref, first_send, first_recv, gain_send, gain_recv, local_sem, send, recv):
    place = Place()
    greet(place)
    me = place.pipe
    mine = dict(place.at)

    def first(q, owner, target):
        return pltpu.make_async_remote_copy(
            src_ref=shard_ref.at[0, q % 2, :, :, pl.ds(pl.multiple_of(q // 2 * (D // 4), 128), D // 4)],
            dst_ref=w_ref.at[owner, q // 2, place.dp // 8, place.dp // 2 % 4, place.core, q % 2],
            send_sem=first_send.at[q],
            recv_sem=first_recv.at[owner],
            device_id=(target, place.dp),
            device_id_type=MESH,
        )

    def gain(owner, q):
        return pltpu.make_async_remote_copy(
            src_ref=gain_ref.at[0],
            dst_ref=gains_ref.at[owner],
            send_sem=gain_send.at[q],
            recv_sem=gain_recv.at[owner],
            device_id=(q, place.dp),
            device_id_type=MESH,
        )

    own = pltpu.make_async_copy(
        shard_ref.at[0, me % 2, :, :, pl.ds(pl.multiple_of(me // 2 * (D // 4), 128), D // 4)],
        w_ref.at[me, me // 2, place.dp // 8, place.dp // 2 % 4, place.core, me % 2],
        local_sem.at[0],
    )
    own_gain = pltpu.make_async_copy(gain_ref.at[0], gains_ref.at[me], local_sem.at[1])
    own.start()
    own_gain.start()
    for q in range(PHASES):
        @pl.when(q != me)
        def _():
            first(q, me, q).start()
            gain(me, q).start()
    for q in range(PHASES):
        @pl.when(q != me)
        def _():
            first(q, me, q).wait_send()
            gain(me, q).wait_send()
            first(q, q, q).wait_recv()
            gain(q, q).wait_recv()
    own.wait()
    own_gain.wait()

    def copies(stage, s, parity):
        made = []

        def add(view, device):
            i = stage_base[stage] + len(made)
            made.append(pltpu.make_async_remote_copy(
                src_ref=view,
                dst_ref=view,
                send_sem=send.at[parity, i],
                recv_sem=recv.at[parity, i],
                device_id=device,
                device_id_type=MESH,
            ))

        if stage == 5:
            add(w_ref.at[s, :, :, :, place.core], place.sibling())
            return made
        for k, (a, b, c) in enumerate(ORDERS):
            def view(**where):
                return block(w_ref, (s,), k, place.core, **{**mine, **where})

            if stage == 0:
                for delta in (1, -1, 2):
                    add(view(), place.neighbour(c, delta))
            elif stage == 1:
                for delta in (1, -1):
                    add(view(**{c: WHOLE}), place.neighbour(b, delta))
            elif stage == 2:
                for h, delta in enumerate((1, -1)):
                    add(view(**{b: place.step(b, -delta), c: half(h)}), place.neighbour(b, delta))
            elif stage == 3:
                for delta in (1, -1):
                    add(view(**{b: WHOLE, c: WHOLE}), place.neighbour(a, delta))
            else:
                for h, delta in enumerate((1, -1)):
                    add(view(**{a: place.step(a, -delta), b: half(h), c: WHOLE}), place.neighbour(a, delta))
        return made

    stage_base = (0, 9, 15, 21, 27, 33)

    def tick(t, carry):
        for stage in range(6):
            s = t - 1 - stage

            @pl.when((s >= 0) & (s < PHASES))
            def _():
                for copy in copies(stage, s, (t + 1) % 2):
                    copy.wait()
        for stage in range(6):
            s = t - stage

            @pl.when((s >= 0) & (s < PHASES))
            def _():
                for copy in copies(stage, s, t % 2):
                    copy.start()
        return carry

    lax.fori_loop(0, PHASES + 6, tick, 0)


def gather(shard, gain_rows):
    anywhere = pl.BlockSpec(memory_space=pl.ANY)
    return pl.pallas_call(
        gather_kernel,
        out_shape=(
            jax.ShapeDtypeStruct((PHASES, *TILES), BF16),
            jax.ShapeDtypeStruct((PHASES, 8, HEAD), F32),
        ),
        in_specs=[anywhere, anywhere],
        out_specs=[anywhere, anywhere],
        scratch_shapes=[
            pltpu.SemaphoreType.DMA((PHASES,)),
            pltpu.SemaphoreType.DMA((PHASES,)),
            pltpu.SemaphoreType.DMA((PHASES,)),
            pltpu.SemaphoreType.DMA((PHASES,)),
            pltpu.SemaphoreType.DMA((2,)),
            pltpu.SemaphoreType.DMA((2, 34)),
            pltpu.SemaphoreType.DMA((2, 34)),
        ],
        compiler_params=pltpu.CompilerParams(collective_id=0, has_side_effects=True),
        name="gather",
    )(shard, gain_rows)


STRIP = (3, 16, D // 4)
STAGE_BASE = (0, 1, 7, 13, 19, 25)
WIDE_PEERS = 16


def cut(ref, lead, k, where):
    index = []
    for axis in ORDERS[k]:
        if axis in where:
            v = where[axis]
            index.append(pl.ds(2 * v[1], 2) if isinstance(v, tuple) else v)
    return ref.at[(*lead, *index)]


def add_into(out, *parts):
    total = parts[0][...].astype(F32)
    for part in parts[1:]:
        total += part[...].astype(F32)
    out[...] = total.astype(out.dtype)


class Scatter:
    def __init__(self, place, bufs):
        self.place = place
        (self.grad, self.pair, self.wide, self.wide_half, self.wide_got, self.slim, self.slim_half,
         self.slim_got, self.last, self.last_got, self.final, self.out, self.send, self.recv,
         self.final_send, self.final_recv) = bufs

    def copies(self, stage, i):
        place, slot = self.place, i % 2
        made = []

        def add(src, dst, device):
            j = STAGE_BASE[stage] + len(made)
            made.append(pltpu.make_async_remote_copy(
                src_ref=src, dst_ref=dst, send_sem=self.send.at[slot, j], recv_sem=self.recv.at[slot, j],
                device_id=device, device_id_type=MESH))

        if stage == 0:
            add(self.grad.at[slot, :, :, :, 1 - place.core], self.pair.at[slot], place.sibling())
            return made
        for k, (a, b, c) in enumerate(ORDERS):
            if stage == 1:
                for h, delta in enumerate((1, -1)):
                    src = cut(self.wide, (slot, k), k, {a: place.step(a, 2), b: half(h)})
                    add(src, self.wide_half.at[slot, k, h], place.neighbour(a, delta))
            elif stage == 2:
                for h, delta in enumerate((1, -1)):
                    src = cut(self.wide, (slot, k), k, {a: place.step(a, delta)})
                    add(src, self.wide_got.at[slot, k, h], place.neighbour(a, delta))
            elif stage == 3:
                for h, delta in enumerate((1, -1)):
                    src = self.slim.at[slot, k, place.step(b, 2), pl.ds(2 * h, 2)]
                    add(src, self.slim_half.at[slot, k, h], place.neighbour(b, delta))
            elif stage == 4:
                for h, delta in enumerate((1, -1)):
                    src = self.slim.at[slot, k, place.step(b, delta)]
                    add(src, self.slim_got.at[slot, k, h], place.neighbour(b, delta))
            else:
                for h, delta in enumerate((1, -1, 2)):
                    src = self.last.at[slot, k, place.step(c, delta)]
                    add(src, self.last_got.at[slot, k, h], place.neighbour(c, delta))
        return made

    def fill_wide(self, i):
        slot = i % 2
        core = self.place.core

        def row(y, carry):
            for xh in range(2):
                for xl in range(2):
                    x = xh * 2 + xl
                    for k in range(3):
                        full = slice(None)
                        where = {"x": x, "y": y, "z": full}
                        out = self.wide.at[(slot, k, *(where[axis] for axis in ORDERS[k]))]
                        add_into(out, self.grad.at[slot, y, xh, :, core, xl, k], self.pair.at[slot, y, xh, :, xl, k])
            return carry

        lax.fori_loop(0, 4, row, 0)

    def process(self, stage, i):
        place, slot = self.place, i % 2
        if stage == 1:
            self.fill_wide(i)
            return
        for k, (a, b, c) in enumerate(ORDERS):
            if stage == 2:
                for h, delta in enumerate((1, -1)):
                    part = self.wide.at[slot, k, place.step(a, delta), pl.ds(2 * h, 2)]
                    add_into(part, part, self.wide_half.at[slot, k, h])
            elif stage == 3:
                add_into(self.slim.at[slot, k], self.wide.at[slot, k, place.at[a]],
                         self.wide_got.at[slot, k, 0], self.wide_got.at[slot, k, 1])
            elif stage == 4:
                for h, delta in enumerate((1, -1)):
                    part = self.slim.at[slot, k, place.step(b, delta), pl.ds(2 * h, 2)]
                    add_into(part, part, self.slim_half.at[slot, k, h])
            elif stage == 5:
                add_into(self.last.at[slot, k], self.slim.at[slot, k, place.at[b]],
                         self.slim_got.at[slot, k, 0], self.slim_got.at[slot, k, 1])
            else:
                add_into(self.final.at[PHASES - 1 - i, k], self.last.at[slot, k, place.at[c]],
                         *(self.last_got.at[slot, k, h] for h in range(3)))

    def final_copy(self, s, source, target):
        return pltpu.make_async_remote_copy(
            src_ref=self.final.at[s], dst_ref=self.out.at[source],
            send_sem=self.final_send.at[s], recv_sem=self.final_recv.at[source],
            device_id=(target, self.place.dp), device_id_type=MESH)

    def deliver(self, i):
        me, s = self.place.pipe, PHASES - 1 - i

        @pl.when(s != me)
        def _():
            self.final_copy(s, me, s).start()

        @pl.when(s == me)
        def _():
            self.out[s] = self.final[s]

    def settle(self):
        for q in range(PHASES):
            @pl.when(q != self.place.pipe)
            def _():
                self.final_copy(q, q, q).wait()

    def tick(self, t, first):
        def each(body, order, lag):
            for stage in order:
                i = t - first - stage - lag

                @pl.when((i >= 0) & (i < PHASES))
                def _():
                    body(stage, i)

        def wait(stage, i):
            for copy in self.copies(stage, i):
                copy.wait()

        def start(stage, i):
            if stage == 6:
                self.deliver(i)
                return
            for copy in self.copies(stage, i):
                copy.start()

        each(wait, range(6), 1)
        each(self.process, (6, 5, 4, 3, 2, 1), 0)
        each(start, range(7), 0)


def scatter_kernel(grads_ref, dgain_ref, out_ref, total_ref, grad, *rest):
    *bufs, gain_rows, gain_wide, gain_sum, gain_send, gain_recv, wide_send, wide_recv, local_sem = rest
    place = Place()
    greet(place, wide=True)
    scatter = Scatter(place, (grad, *bufs))
    me = place.pipe

    def gain(owner, source, target):
        return pltpu.make_async_remote_copy(
            src_ref=dgain_ref.at[owner], dst_ref=gain_rows.at[source],
            send_sem=gain_send.at[owner], recv_sem=gain_recv.at[source],
            device_id=(target, place.dp), device_id_type=MESH)

    def gain_share(index, source, target):
        return pltpu.make_async_remote_copy(
            src_ref=gain_sum, dst_ref=gain_wide.at[source],
            send_sem=wide_send.at[index], recv_sem=wide_recv.at[source],
            device_id=(me, target), device_id_type=MESH)

    for q in range(PHASES):
        @pl.when(q != me)
        def _():
            gain(q, me, q).start()

        @pl.when(q == me)
        def _():
            gain_rows[q] = dgain_ref[q]
    for q in range(PHASES):
        @pl.when(q != me)
        def _():
            gain(q, q, q).wait()
    gain_sum[...] = jnp.sum(gain_rows[...], axis=0)
    for q in range(WIDE_PEERS):
        @pl.when(q != place.dp)
        def _():
            gain_share(q, place.dp, q).start()

        @pl.when(q == place.dp)
        def _():
            gain_wide[q] = gain_sum[...]

    def load(i):
        return pltpu.make_async_copy(grads_ref.at[PHASES - 1 - i], grad.at[i % 2], local_sem.at[i % 2])

    def tick(t, carry):
        @pl.when((t >= 1) & (t <= PHASES))
        def _():
            load(t - 1).wait()

        scatter.tick(t, 1)

        @pl.when(t < PHASES)
        def _():
            load(t).start()

        return carry

    lax.fori_loop(0, PHASES + 7, tick, 0)
    for q in range(WIDE_PEERS):
        @pl.when(q != place.dp)
        def _():
            gain_share(q, q, q).wait()
    total_ref[...] = jnp.sum(gain_wide[...], axis=0)
    scatter.settle()
    for y in range(4):
        for xl in range(2):
            out_ref[xl, :, :, pl.ds(y * (D // 4), D // 4)] = scatter.out[y * 2 + xl].astype(F32)


def scatter_scratch():
    piece = (16, D // 4)
    sems = pltpu.SemaphoreType.DMA
    return [
        pltpu.VMEM((2, *TILES), BF16),
        pltpu.VMEM((2, 4, 2, 4, 2, *STRIP), BF16),
        pltpu.VMEM((2, 3, 4, 4, 4, *piece), BF16),
        pltpu.VMEM((2, 3, 2, 2, 4, *piece), BF16),
        pltpu.VMEM((2, 3, 2, 4, 4, *piece), BF16),
        pltpu.VMEM((2, 3, 4, 4, *piece), BF16),
        pltpu.VMEM((2, 3, 2, 2, *piece), BF16),
        pltpu.VMEM((2, 3, 2, 4, *piece), BF16),
        pltpu.VMEM((2, 3, 4, *piece), BF16),
        pltpu.VMEM((2, 3, 3, *piece), BF16),
        pltpu.VMEM((PHASES, *STRIP), BF16),
        pltpu.VMEM((PHASES, *STRIP), BF16),
        sems((2, 34)),
        sems((2, 34)),
        sems((PHASES,)),
        sems((PHASES,)),
        pltpu.VMEM((PHASES, 8, HEAD), F32),
        pltpu.VMEM((WIDE_PEERS, 8, HEAD), F32),
        pltpu.VMEM((8, HEAD), F32),
        sems((PHASES,)),
        sems((PHASES,)),
        sems((WIDE_PEERS,)),
        sems((WIDE_PEERS,)),
        sems((2,)),
    ]


def scatter(grads, dgains):
    return pl.pallas_call(
        scatter_kernel,
        out_shape=(
            jax.ShapeDtypeStruct((2, 3, 16, D), F32),
            jax.ShapeDtypeStruct((8, HEAD), F32),
        ),
        in_specs=[pl.BlockSpec(memory_space=pl.ANY), pl.BlockSpec(memory_space=pltpu.VMEM)],
        out_specs=[pl.BlockSpec(memory_space=pltpu.VMEM)] * 2,
        scratch_shapes=scatter_scratch(),
        compiler_params=pltpu.CompilerParams(
            collective_id=1, has_side_effects=True, vmem_limit_bytes=60 << 20
        ),
        name="scatter",
    )(grads, dgains)


def head(j):
    return pl.ds(j * HEAD, HEAD)


def forward_phase(s, w_ref, tabs, swap, hs, qs, ks, es, ms, ns, rcols, icols):
    a0, b0, a1, b1 = tabs
    ones = jnp.ones((TOK, HEAD), BF16)
    for j in range(HEADS):
        hj = hs[s, :, head(j)]
        hf = hj.astype(F32)
        r = lax.rsqrt(jnp.mean(hf * hf, axis=-1, keepdims=True) + 1e-6)
        rcols[s, :, j : j + 1] = r
        n = hf * r
        nsw = dot(hj, swap) * r
        ns[s, :, head(j)] = nsw.astype(BF16)
        qs[s, :, head(j)] = (n * a0 + nsw * b0).astype(BF16)
        ks[s, :, head(j)] = (n * a1 + nsw * b1).astype(BF16)
    for j in range(HEADS):
        scores = dot(qs[s, :, head(j)], ks[s, :, head(j)], NT)
        es[s, :, head(j)] = jnp.exp(scores).astype(BF16)
    for j in range(HEADS):
        both = dot(es[s, :, head(j)], jnp.concatenate([hs[s, :, head(j)], ones], axis=1))
        inv = 1.0 / both[:, HEAD:]
        icols[s, :, j : j + 1] = inv[:, 0:1]
        ms[s, :, head(j)] = (both[:, :HEAD] * inv).astype(BF16)
    for c in range(4):
        cols = pl.ds(c * 384, 384)
        update = dot(ms[s], w_ref[0, c])
        hs[s + 1, :, cols] = (hs[s, :, cols].astype(F32) + update).astype(BF16)


def backward_phase(s, w_ref, tabs, swap, g, gm, acc, hs, qs, ks, es, ms, ns, rcols, icols, grad_ref):
    a0, b0, a1, b1 = tabs
    for c in range(D // 512):
        cols = pl.ds(c * 512, 512)
        total = dot(g[:, 0:384], w_ref[0, 0, cols, :], NT)
        for y in range(1, 4):
            total += dot(g[:, pl.ds(y * 384, 384)], w_ref[0, y, cols, :], NT)
        gm[:, cols] = total.astype(BF16)
    for y in range(4):
        cols = pl.ds(y * 384, 384)
        for t in range(D // 512):
            rows = pl.ds(t * 512, 512)
            grad_ref[0, y, rows] = dot(ms[s, :, rows], g[:, cols], TN).astype(BF16)
    acc[...] = jnp.zeros_like(acc)
    for j in range(HEADS):
        hj = hs[s, :, head(j)]
        ej = es[s, :, head(j)]
        qj = qs[s, :, head(j)]
        kj = ks[s, :, head(j)]
        r = rcols[s, :, j : j + 1]
        gmf = gm[:, head(j)].astype(F32) * icols[s, :, j : j + 1]
        delta = jnp.sum(gmf * ms[s, :, head(j)].astype(F32), axis=-1, keepdims=True)
        gmb = gmf.astype(BF16)
        ga = dot(gmb, hj, NT)
        ds = (ej.astype(F32) * (ga - delta)).astype(BF16)
        gv = dot(ej, gmb, TN)
        dq = dot(ds, kj)
        dk = dot(ds, qj, TN)
        n = hj.astype(F32) * r
        nsw = ns[s, :, head(j)].astype(F32)
        acc[0] += n * dq
        acc[1] += nsw * dq
        acc[2] += n * dk
        acc[3] += nsw * dk
        crossed = (dq * b0 + dk * b1).astype(BF16)
        dn = dq * a0 + dk * a1 + dot(crossed, swap, NT)
        dh = r * (dn - n * jnp.mean(dn * n, axis=-1, keepdims=True))
        g[:, head(j)] = (g[:, head(j)].astype(F32) + (dh + gv)).astype(BF16)


def compute_kernel(place_ref, clip_ref, pos_ref, cot_ref, gains_ref, freq_ref, swap_ref, sign_ref, w_ref,
                   grad_ref, dgain_ref, hs, qs, ks, es, ms, ns, rcols, icols, g, gm, acc, cosine, sine):
    step = pl.program_id(0)
    live = place_ref[0] < 6
    scale = 1.0 / math.sqrt(HEAD)
    swap = swap_ref[...]

    def tables(s):
        rows = gains_ref[s]
        c, n = cosine[...], sine[...]
        return (c * (rows[0:1] * scale), n * (rows[2:3] * scale), c * rows[1:2], n * rows[3:4])

    saved = (hs, qs, ks, es, ms, ns, rcols, icols)

    @pl.when(live & (step == 0))
    def _():
        p = place_ref[0]
        positions = pos_ref[:, p // 3, p % 3, :].astype(F32)
        padded = jnp.concatenate([positions, jnp.zeros((5, TOK), F32)], axis=0)
        angles = dot(padded, freq_ref[...], TN, lax.Precision.HIGHEST)
        cosine[...] = jnp.cos(angles)
        sine[...] = jnp.sin(angles) * sign_ref[...]
        hs[0] = clip_ref[0, 0]

    @pl.when(live & (step < PHASES))
    def _():
        forward_phase(step, w_ref, tables(step), swap, *saved)

    @pl.when(live & (step == PHASES))
    def _():
        g[...] = cot_ref[0, 0]

    @pl.when(live & (step >= PHASES))
    def _():
        s = 2 * PHASES - 1 - step
        backward_phase(s, w_ref, tables(s), swap, g, gm, acc, *saved, grad_ref)
        x0 = jnp.sum(acc[0] * cosine[...], axis=0, keepdims=True)
        y0 = jnp.sum(acc[1] * sine[...], axis=0, keepdims=True)
        x1 = jnp.sum(acc[2] * cosine[...], axis=0, keepdims=True)
        y1 = jnp.sum(acc[3] * sine[...], axis=0, keepdims=True)
        rows = jnp.concatenate([x0 * scale, x1, y0 * scale, y1, jnp.zeros((4, HEAD), F32)], axis=0)
        dgain_ref[0] = rows

    @pl.when(jnp.logical_not(live) & (step >= PHASES))
    def _():
        grad_ref[...] = jnp.zeros_like(grad_ref)
        dgain_ref[...] = jnp.zeros_like(dgain_ref)


def compute(place, clips, positions, cotangent, gains, weights):
    freq, swap, sign = rotary_constants()

    def group(i, place_ref):
        p = jnp.minimum(place_ref[0], 5)
        return (p // 3, p % 3)

    def phase_of(i):
        return jnp.minimum(i, 2 * PHASES - 1 - i)

    def out_phase(i):
        return jnp.minimum(2 * PHASES - 1 - i, PHASES - 1)

    whole = lambda rank: (lambda i, p: (0,) * rank)
    spec = pltpu.PrefetchScalarGridSpec(
        num_scalar_prefetch=1,
        grid=(2 * PHASES,),
        in_specs=[
            pl.BlockSpec((1, 1, TOK, D), lambda i, p: (*group(i, p), 0, 0)),
            pl.BlockSpec((3, 2, 3, TOK), whole(4)),
            pl.BlockSpec((1, 1, TOK, D), lambda i, p: (*group(i, p), 0, 0)),
            pl.BlockSpec((PHASES, 8, HEAD), whole(3)),
            pl.BlockSpec((8, HEAD), whole(2)),
            pl.BlockSpec((HEAD, HEAD), whole(2)),
            pl.BlockSpec((1, HEAD), whole(2)),
            pl.BlockSpec((1, 4, D, D // 4), lambda i, p: (phase_of(i), 0, 0, 0)),
        ],
        out_specs=[
            pl.BlockSpec((1, 4, D, D // 4), lambda i, p: (out_phase(i), 0, 0, 0)),
            pl.BlockSpec((1, 8, HEAD), lambda i, p: (out_phase(i), 0, 0)),
        ],
        scratch_shapes=[
            pltpu.VMEM((PHASES + 1, TOK, D), BF16),
            pltpu.VMEM((PHASES, TOK, D), BF16),
            pltpu.VMEM((PHASES, TOK, D), BF16),
            pltpu.VMEM((PHASES, TOK, D), BF16),
            pltpu.VMEM((PHASES, TOK, D), BF16),
            pltpu.VMEM((PHASES, TOK, D), BF16),
            pltpu.VMEM((PHASES, TOK, HEAD), F32),
            pltpu.VMEM((PHASES, TOK, HEAD), F32),
            pltpu.VMEM((TOK, D), BF16),
            pltpu.VMEM((TOK, D), BF16),
            pltpu.VMEM((4, TOK, HEAD), F32),
            pltpu.VMEM((TOK, HEAD), F32),
            pltpu.VMEM((TOK, HEAD), F32),
        ],
    )
    return pl.pallas_call(
        compute_kernel,
        grid_spec=spec,
        out_shape=(
            jax.ShapeDtypeStruct((PHASES, 4, D, D // 4), BF16),
            jax.ShapeDtypeStruct((PHASES, 8, HEAD), F32),
        ),
        compiler_params=pltpu.CompilerParams(
            dimension_semantics=("arbitrary",), vmem_limit_bytes=60 << 20
        ),
        name="phases",
    )(
        place, clips, positions, cotangent, gains, jnp.asarray(freq),
        jnp.asarray(swap, BF16), jnp.asarray(sign), weights,
    )


def shards(clips, positions, out_proj, qk_gains, cotangent):
    place = lax.axis_index("pipe")
    _, swap, _ = rotary_constants()
    partner = np.argmax(swap, axis=0)
    own = qk_gains[0].astype(F32)
    gain_rows = jnp.concatenate([own, own[:, partner], jnp.zeros((4, HEAD), F32)], axis=0)[None]
    tiles, gains = gather(out_proj.reshape(1, 2, 3, 16, D), gain_rows)
    weights = tiles.reshape(PHASES, 4, D, D // 4)
    grads, dgains = compute(place[None], clips, positions, cotangent, gains, weights)
    shard, total = scatter(grads.reshape(PHASES, *TILES), dgains)
    dgain = total[0:2] + total[2:4][:, partner]
    return (shard.reshape(1, D // 16, D), dgain[None])


def solution(mesh):
    placed = (
        P(None, None, "dp", None),
        P(None, None, None, "dp"),
        P("pipe", "dp", None),
        P("pipe", None, None),
        P(None, None, "dp", None),
    )
    return jax.shard_map(
        shards,
        mesh=mesh,
        in_specs=placed,
        out_specs=(P("pipe", "dp", None), P("pipe", None, None)),
        check_vma=False,
    )
```

```python
import functools
import math

import jax
import jax.numpy as jnp
import numpy as np
from jax import lax
from jax.experimental import pallas as pl
from jax.experimental.pallas import tpu as pltpu
from jax.sharding import PartitionSpec as P

D = 1536
HEAD = 128
TOK = 128
HEADS = D // HEAD
PHASES = 8
F32 = jnp.float32
BF16 = jnp.bfloat16

NN = (((1,), (0,)), ((), ()))
NT = (((1,), (1,)), ((), ()))
TN = (((0,), (0,)), ((), ()))


def dot(a, b, dims=NN, precision=None):
    return lax.dot_general(a, b, dims, precision=precision, preferred_element_type=F32)


def rotary_constants():
    first = HEAD // 8
    rest = (HEAD - first) // 2
    freq = np.zeros((8, HEAD), np.float32)
    partner = np.zeros(HEAD, np.int32)
    sign = np.zeros((1, HEAD), np.float32)
    offset = 0
    for axis, width in enumerate((first, rest, rest)):
        half = width // 2
        values = np.float32(256.0) ** (np.float32(-2.0) * np.arange(half, dtype=np.float32) / np.float32(width))
        low = np.arange(offset, offset + half)
        high = low + half
        freq[axis, low] = values
        freq[axis, high] = values
        partner[low], partner[high] = high, low
        sign[0, low], sign[0, high] = -1.0, 1.0
        offset += width
    swap = np.zeros((HEAD, HEAD), np.float32)
    swap[partner, np.arange(HEAD)] = 1.0
    return freq, swap, sign


MESH = pl.DeviceIdType.MESH
AXES = "xyz"
GATHER_LAG = 2
GATHER_BASE = (0, 9, 15, 21, 27, 33)
ORDERS = ("xyz", "yzx", "zxy")


class Place:
    def __init__(self):
        self.pipe = lax.axis_index("pipe")
        self.dp = lax.axis_index("dp")
        self.core = self.dp % 2
        self.at = {
            "x": self.dp // 8 * 2 + self.pipe % 2,
            "y": self.pipe // 2,
            "z": self.dp // 2 % 4,
        }

    def device(self, core=None, **moved):
        c = {**self.at, **moved}
        core = self.core if core is None else core
        return (c["y"] * 2 + c["x"] % 2, (c["x"] // 2 * 4 + c["z"]) * 2 + core)

    def step(self, axis, delta):
        return (self.at[axis] + delta + 4) % 4

    def neighbour(self, axis, delta):
        return self.device(**{axis: self.step(axis, delta)})

    def sibling(self):
        return self.device(core=1 - self.core)


def greet(place):
    barrier = pltpu.get_barrier_semaphore()
    others = [place.neighbour(axis, delta) for axis in AXES for delta in (1, -1, 2)]
    others.append(place.sibling())
    others += [((place.pipe + q) % PHASES, place.dp) for q in range(1, PHASES)]
    others += [(place.pipe, (place.dp + q) % WIDE_PEERS) for q in range(1, WIDE_PEERS)]
    for other in others:
        pl.semaphore_signal(barrier, inc=1, device_id=other, device_id_type=MESH)
    pl.semaphore_wait(barrier, len(others))


WHOLE = "whole"


def half(h):
    return ("half", h)


def block(ref, lead, k, core, x, y, z):
    def plain(v):
        if v is WHOLE:
            return slice(None)
        return pl.ds(2 * v[1], 2) if isinstance(v, tuple) else v

    if x is WHOLE:
        xh, xl = slice(None), slice(None)
    elif isinstance(x, tuple):
        xh, xl = x[1], slice(None)
    else:
        xh, xl = x // 2, x % 2
    return ref.at[(*lead, plain(y), xh, plain(z), core, xl, k)]


TILES = (4, 2, 4, 2, 2, 3, 16, D // 4)


class Gather:
    def __init__(self, place, shard, gain, weights, gains, sems):
        self.place, self.shard, self.gain, self.weights, self.gains = place, shard, gain, weights, gains
        (self.first_send, self.first_recv, self.gain_send, self.gain_recv, self.own_sem, self.send, self.recv) = sems

    def piece(self, q):
        return self.shard.at[0, q % 2, :, :, pl.ds(pl.multiple_of(q // 2 * (D // 4), 128), D // 4)]

    def spot(self, owner, q):
        place = self.place
        return self.weights.at[owner, q // 2, place.dp // 8, place.dp // 2 % 4, place.core, q % 2]

    def first(self, q, owner, target):
        return pltpu.make_async_remote_copy(
            src_ref=self.piece(q), dst_ref=self.spot(owner, q),
            send_sem=self.first_send.at[q], recv_sem=self.first_recv.at[owner],
            device_id=(target, self.place.dp), device_id_type=MESH)

    def gain_copy(self, owner, q):
        return pltpu.make_async_remote_copy(
            src_ref=self.gain.at[0], dst_ref=self.gains.at[owner],
            send_sem=self.gain_send.at[q], recv_sem=self.gain_recv.at[owner],
            device_id=(q, self.place.dp), device_id_type=MESH)

    def spread(self):
        me = self.place.pipe
        own = pltpu.make_async_copy(self.piece(me), self.spot(me, me), self.own_sem.at[0])
        own.start()
        for q in range(PHASES):
            @pl.when(q != me)
            def _():
                self.first(q, me, q).start()
                self.gain_copy(me, q).start()

            @pl.when(q == me)
            def _():
                self.gains[q] = self.gain[0]
        own.wait()

    def spread_wait(self):
        for q in range(PHASES):
            @pl.when(q != self.place.pipe)
            def _():
                self.first(q, self.place.pipe, q).wait_send()
                self.gain_copy(self.place.pipe, q).wait_send()
                self.first(q, q, q).wait_recv()
                self.gain_copy(q, q).wait_recv()

    def copies(self, stage, s, parity):
        place = self.place
        made = []

        def add(view, device):
            i = GATHER_BASE[stage] + len(made)
            made.append(pltpu.make_async_remote_copy(
                src_ref=view, dst_ref=view, send_sem=self.send.at[parity, i], recv_sem=self.recv.at[parity, i],
                device_id=device, device_id_type=MESH))

        if stage == 5:
            add(self.weights.at[s, :, :, :, place.core], place.sibling())
            return made
        for k, (a, b, c) in enumerate(ORDERS):
            def view(**where):
                return block(self.weights, (s,), k, place.core, **{**place.at, **where})

            if stage == 0:
                for delta in (1, -1, 2):
                    add(view(), place.neighbour(c, delta))
            elif stage == 1:
                for delta in (1, -1):
                    add(view(**{c: WHOLE}), place.neighbour(b, delta))
            elif stage == 2:
                for h, delta in enumerate((1, -1)):
                    add(view(**{b: place.step(b, -delta), c: half(h)}), place.neighbour(b, delta))
            elif stage == 3:
                for delta in (1, -1):
                    add(view(**{b: WHOLE, c: WHOLE}), place.neighbour(a, delta))
            else:
                for h, delta in enumerate((1, -1)):
                    add(view(**{a: place.step(a, -delta), b: half(h), c: WHOLE}), place.neighbour(a, delta))
        return made

    def tick(self, t):
        for stage in reversed(range(7)):
            s = t - GATHER_LAG * stage

            @pl.when((s >= 0) & (s < PHASES))
            def _():
                if stage:
                    for copy in self.copies(stage - 1, s, (t + GATHER_LAG) % (2 * GATHER_LAG)):
                        copy.wait()
                if stage < 6:
                    for copy in self.copies(stage, s, t % (2 * GATHER_LAG)):
                        copy.start()


STRIP = (3, 16, D // 4)
STAGE_BASE = (0, 1, 7, 13, 19, 25)
WIDE_PEERS = 16


def cut(ref, lead, k, where):
    index = []
    for axis in ORDERS[k]:
        if axis in where:
            v = where[axis]
            index.append(pl.ds(2 * v[1], 2) if isinstance(v, tuple) else v)
    return ref.at[(*lead, *index)]


def add_into(out, *parts):
    total = parts[0][...].astype(F32)
    for part in parts[1:]:
        total += part[...].astype(F32)
    out[...] = total.astype(out.dtype)


class Scatter:
    def __init__(self, place, bufs):
        self.place = place
        (self.grad, self.pair, self.wide, self.wide_half, self.wide_got, self.slim, self.slim_half,
         self.slim_got, self.last, self.last_got, self.final, self.out, self.send, self.recv,
         self.final_send, self.final_recv) = bufs

    def copies(self, stage, i):
        place, slot = self.place, i % 2
        made = []

        def add(src, dst, device):
            j = STAGE_BASE[stage] + len(made)
            made.append(pltpu.make_async_remote_copy(
                src_ref=src, dst_ref=dst, send_sem=self.send.at[slot, j], recv_sem=self.recv.at[slot, j],
                device_id=device, device_id_type=MESH))

        if stage == 0:
            add(self.grad.at[slot, :, :, :, 1 - place.core], self.pair.at[slot], place.sibling())
            return made
        for k, (a, b, c) in enumerate(ORDERS):
            if stage == 1:
                for h, delta in enumerate((1, -1)):
                    src = cut(self.wide, (slot, k), k, {a: place.step(a, 2), b: half(h)})
                    add(src, self.wide_half.at[slot, k, h], place.neighbour(a, delta))
            elif stage == 2:
                for h, delta in enumerate((1, -1)):
                    src = cut(self.wide, (slot, k), k, {a: place.step(a, delta)})
                    add(src, self.wide_got.at[slot, k, h], place.neighbour(a, delta))
            elif stage == 3:
                for h, delta in enumerate((1, -1)):
                    src = self.slim.at[slot, k, place.step(b, 2), pl.ds(2 * h, 2)]
                    add(src, self.slim_half.at[slot, k, h], place.neighbour(b, delta))
            elif stage == 4:
                for h, delta in enumerate((1, -1)):
                    src = self.slim.at[slot, k, place.step(b, delta)]
                    add(src, self.slim_got.at[slot, k, h], place.neighbour(b, delta))
            else:
                for h, delta in enumerate((1, -1, 2)):
                    src = self.last.at[slot, k, place.step(c, delta)]
                    add(src, self.last_got.at[slot, k, h], place.neighbour(c, delta))
        return made

    def fill_wide(self, i):
        slot = i % 2
        core = self.place.core

        def row(y, carry):
            for xh in range(2):
                for xl in range(2):
                    x = xh * 2 + xl
                    for k in range(3):
                        full = slice(None)
                        where = {"x": x, "y": y, "z": full}
                        out = self.wide.at[(slot, k, *(where[axis] for axis in ORDERS[k]))]
                        add_into(out, self.grad.at[slot, y, xh, :, core, xl, k], self.pair.at[slot, y, xh, :, xl, k])
            return carry

        lax.fori_loop(0, 4, row, 0)

    def process(self, stage, i):
        place, slot = self.place, i % 2
        if stage == 1:
            self.fill_wide(i)
            return
        for k, (a, b, c) in enumerate(ORDERS):
            if stage == 2:
                for h, delta in enumerate((1, -1)):
                    part = self.wide.at[slot, k, place.step(a, delta), pl.ds(2 * h, 2)]
                    add_into(part, part, self.wide_half.at[slot, k, h])
            elif stage == 3:
                add_into(self.slim.at[slot, k], self.wide.at[slot, k, place.at[a]],
                         self.wide_got.at[slot, k, 0], self.wide_got.at[slot, k, 1])
            elif stage == 4:
                for h, delta in enumerate((1, -1)):
                    part = self.slim.at[slot, k, place.step(b, delta), pl.ds(2 * h, 2)]
                    add_into(part, part, self.slim_half.at[slot, k, h])
            elif stage == 5:
                add_into(self.last.at[slot, k], self.slim.at[slot, k, place.at[b]],
                         self.slim_got.at[slot, k, 0], self.slim_got.at[slot, k, 1])
            else:
                add_into(self.final.at[PHASES - 1 - i, k], self.last.at[slot, k, place.at[c]],
                         *(self.last_got.at[slot, k, h] for h in range(3)))

    def final_copy(self, s, source, target):
        return pltpu.make_async_remote_copy(
            src_ref=self.final.at[s], dst_ref=self.out.at[source],
            send_sem=self.final_send.at[s], recv_sem=self.final_recv.at[source],
            device_id=(target, self.place.dp), device_id_type=MESH)

    def deliver(self, i):
        me, s = self.place.pipe, PHASES - 1 - i

        @pl.when(s != me)
        def _():
            self.final_copy(s, me, s).start()

        @pl.when(s == me)
        def _():
            self.out[s] = self.final[s]

    def settle(self):
        for q in range(PHASES):
            @pl.when(q != self.place.pipe)
            def _():
                self.final_copy(q, q, q).wait()

    def tick(self, t, first):
        for stage in reversed(range(7)):
            i = t - first - stage

            @pl.when((i >= 0) & (i < PHASES))
            def _():
                if stage:
                    for copy in self.copies(stage - 1, i):
                        copy.wait()
                    self.process(stage, i)
                if stage < 6:
                    for copy in self.copies(stage, i):
                        copy.start()
                else:
                    self.deliver(i)


class GainSum:
    def __init__(self, place, dgains, bufs):
        self.place, self.dgains = place, dgains
        (self.rows, self.wide, self.sum, self.send, self.recv, self.wide_send, self.wide_recv) = bufs

    def narrow(self, owner, source, target):
        return pltpu.make_async_remote_copy(
            src_ref=self.dgains.at[owner], dst_ref=self.rows.at[source],
            send_sem=self.send.at[owner], recv_sem=self.recv.at[source],
            device_id=(target, self.place.dp), device_id_type=MESH)

    def share(self, index, source, target):
        return pltpu.make_async_remote_copy(
            src_ref=self.sum, dst_ref=self.wide.at[source],
            send_sem=self.wide_send.at[index], recv_sem=self.wide_recv.at[source],
            device_id=(self.place.pipe, target), device_id_type=MESH)

    def start(self):
        me = self.place.pipe
        for q in range(PHASES):
            @pl.when(q != me)
            def _():
                self.narrow(q, me, q).start()

            @pl.when(q == me)
            def _():
                self.rows[q] = self.dgains[q]

    def middle(self):
        for q in range(PHASES):
            @pl.when(q != self.place.pipe)
            def _():
                self.narrow(q, q, q).wait()
        self.sum[...] = jnp.sum(self.rows[...], axis=0)
        for q in range(WIDE_PEERS):
            @pl.when(q != self.place.dp)
            def _():
                self.share(q, self.place.dp, q).start()

            @pl.when(q == self.place.dp)
            def _():
                self.wide[q] = self.sum[...]

    def finish(self, total):
        for q in range(WIDE_PEERS):
            @pl.when(q != self.place.dp)
            def _():
                self.share(q, q, q).wait()
        total[...] = jnp.sum(self.wide[...], axis=0)


def head(j):
    return pl.ds(j * HEAD, HEAD)


def forward_phase(s, w_ref, tabs, swap, hs, qs, ks, es, ms, ns, rcols, icols):
    a0, b0, a1, b1 = tabs
    ones = jnp.ones((TOK, HEAD), BF16)
    for j in range(HEADS):
        hj = hs[s, :, head(j)]
        hf = hj.astype(F32)
        r = lax.rsqrt(jnp.mean(hf * hf, axis=-1, keepdims=True) + 1e-6)
        rcols[s, :, j : j + 1] = r
        n = hf * r
        nsw = dot(hj, swap) * r
        ns[s, :, head(j)] = nsw.astype(BF16)
        qs[s, :, head(j)] = (n * a0 + nsw * b0).astype(BF16)
        ks[s, :, head(j)] = (n * a1 + nsw * b1).astype(BF16)
    for j in range(HEADS):
        scores = dot(qs[s, :, head(j)], ks[s, :, head(j)], NT)
        es[s, :, head(j)] = jnp.exp(scores).astype(BF16)
    for j in range(HEADS):
        both = dot(es[s, :, head(j)], jnp.concatenate([hs[s, :, head(j)], ones], axis=1))
        inv = 1.0 / both[:, HEAD:]
        icols[s, :, j : j + 1] = inv[:, 0:1]
        ms[s, :, head(j)] = (both[:, :HEAD] * inv).astype(BF16)
    for c in range(4):
        cols = pl.ds(c * 384, 384)
        update = dot(ms[s], w_ref[s % 2, c].reshape(D, D // 4))
        hs[s + 1, :, cols] = (hs[s, :, cols].astype(F32) + update).astype(BF16)


def backward_phase(s, w_ref, tabs, swap, g, gm, acc, hs, qs, ks, es, ms, ns, rcols, icols, grad_ref):
    a0, b0, a1, b1 = tabs
    for c in range(4):
        cols = pl.ds(c * 384, 384)
        total = None
        for y in range(4):
            part = dot(g[:, pl.ds(y * 384, 384)], w_ref[s % 2, y, c // 2, pl.ds(c % 2 * 2, 2)].reshape(384, D // 4), NT)
            total = part if total is None else total + part
        gm[:, cols] = total.astype(BF16)
    for y in range(4):
        cols = pl.ds(y * 384, 384)
        for t in range(4):
            rows = pl.ds(t * 384, 384)
            part = dot(ms[s, :, rows], g[:, cols], TN).astype(BF16)
            grad_ref[(s + 1) % 2, y, t // 2, pl.ds(t % 2 * 2, 2)] = part.reshape(2, 2, 2, *STRIP)
    acc[...] = jnp.zeros_like(acc)
    for j in range(HEADS):
        hj = hs[s, :, head(j)]
        ej = es[s, :, head(j)]
        qj = qs[s, :, head(j)]
        kj = ks[s, :, head(j)]
        r = rcols[s, :, j : j + 1]
        gmf = gm[:, head(j)].astype(F32) * icols[s, :, j : j + 1]
        delta = jnp.sum(gmf * ms[s, :, head(j)].astype(F32), axis=-1, keepdims=True)
        gmb = gmf.astype(BF16)
        ga = dot(gmb, hj, NT)
        ds = (ej.astype(F32) * (ga - delta)).astype(BF16)
        gv = dot(ej, gmb, TN)
        dq = dot(ds, kj)
        dk = dot(ds, qj, TN)
        n = hj.astype(F32) * r
        nsw = ns[s, :, head(j)].astype(F32)
        acc[0] += n * dq
        acc[1] += nsw * dq
        acc[2] += n * dk
        acc[3] += nsw * dk
        crossed = (dq * b0 + dk * b1).astype(BF16)
        dn = dq * a0 + dk * a1 + dot(crossed, swap, NT)
        dh = r * (dn - n * jnp.mean(dn * n, axis=-1, keepdims=True))
        g[:, head(j)] = (g[:, head(j)].astype(F32) + (dh + gv)).astype(BF16)


LIVE = 6


def window_kernel(shard_ref, gain_ref, clip_ref, pos_ref, cot_ref, freq_ref, swap_ref, sign_ref,
                  w_ref, out_ref, total_ref, *rest):
    rest = iter(rest)
    take = lambda count: [next(rest) for _ in range(count)]
    saved = take(8)
    g, gm, acc, cosine, sine, gains, dgains, wbuf = take(8)
    gather_sems = take(7)
    scatter_bufs = take(16)
    gain_bufs = take(7)
    in_sem, w_sem = take(2)
    grad = scatter_bufs[0]
    hs = saved[0]
    place = Place()
    live = place.pipe < LIVE
    slot = jnp.minimum(place.pipe, LIVE - 1)
    clip_in = pltpu.make_async_copy(clip_ref.at[slot // 3, slot % 3], hs.at[0], in_sem.at[0])
    cot_in = pltpu.make_async_copy(cot_ref.at[slot // 3, slot % 3], g, in_sem.at[1])
    clip_in.start()
    cot_in.start()
    greet(place)
    gather = Gather(place, shard_ref, gain_ref, w_ref, gains, gather_sems)
    scatter = Scatter(place, scatter_bufs)
    sums = GainSum(place, dgains, gain_bufs)
    scale = 1.0 / math.sqrt(HEAD)
    gather.spread()
    positions = pos_ref[:, slot // 3, slot % 3, :].astype(F32)
    padded = jnp.concatenate([positions, jnp.zeros((5, TOK), F32)], axis=0)
    angles = dot(padded, freq_ref[...], TN, lax.Precision.HIGHEST)
    cosine[...] = jnp.cos(angles)
    sine[...] = jnp.sin(angles) * sign_ref[...]

    @pl.when(jnp.logical_not(live))
    def _():
        grad[...] = jnp.zeros_like(grad)
        dgains[...] = jnp.zeros_like(dgains)

    clip_in.wait()
    cot_in.wait()
    gather.spread_wait()

    def tables(s):
        rows = gains[s]
        c, n = cosine[...], sine[...]
        return (c * (rows[0:1] * scale), n * (rows[2:3] * scale), c * rows[1:2], n * rows[3:4])

    def weights_in(s):
        return pltpu.make_async_copy(w_ref.at[s], wbuf.at[s % 2], w_sem.at[s % 2])

    arrive = 6 * GATHER_LAG

    def forward_tick(t, carry):
        gather.tick(t)
        s = t - arrive - 1

        @pl.when(s >= 0)
        def _():
            weights_in(s).wait()

            @pl.when(live)
            def _():
                forward_phase(s, wbuf, tables(s), swap_ref[...], *saved)

        ready = t - arrive

        @pl.when((ready >= 0) & (ready < PHASES))
        def _():
            weights_in(ready).start()

        return carry

    lax.fori_loop(0, PHASES + arrive + 1, forward_tick, 0)

    def backward_tick(t, carry):
        scatter.tick(t, 1)
        s = PHASES - 1 - t

        @pl.when((t >= 2) & (t < PHASES))
        def _():
            weights_in(s).wait()

        @pl.when(live & (t < PHASES))
        def _():
            backward_phase(s, wbuf, tables(s), swap_ref[...], g, gm, acc, *saved, grad)
            x0 = jnp.sum(acc[0] * cosine[...], axis=0, keepdims=True)
            y0 = jnp.sum(acc[1] * sine[...], axis=0, keepdims=True)
            x1 = jnp.sum(acc[2] * cosine[...], axis=0, keepdims=True)
            y1 = jnp.sum(acc[3] * sine[...], axis=0, keepdims=True)
            dgains[s] = jnp.concatenate([x0 * scale, x1, y0 * scale, y1, jnp.zeros((4, HEAD), F32)], axis=0)

        @pl.when(t < PHASES - 2)
        def _():
            weights_in(s - 2).start()

        @pl.when(t == PHASES)
        def _():
            sums.start()

        @pl.when(t == PHASES + 2)
        def _():
            sums.middle()

        return carry

    lax.fori_loop(0, PHASES + 7, backward_tick, 0)
    sums.finish(total_ref)
    scatter.settle()
    for y in range(4):
        for xl in range(2):
            out_ref[xl, :, :, pl.ds(y * (D // 4), D // 4)] = scatter.out[y * 2 + xl].astype(F32)


def window(shard, gain_rows, clips, positions, cotangent):
    freq, swap, sign = rotary_constants()
    piece = (16, D // 4)
    sems = pltpu.SemaphoreType.DMA
    vmem = pl.BlockSpec(memory_space=pltpu.VMEM)
    anywhere = pl.BlockSpec(memory_space=pl.ANY)
    rows = pltpu.VMEM((PHASES, TOK, D), BF16)
    columns = pltpu.VMEM((PHASES, TOK, HEAD), F32)
    scratch = [
        pltpu.VMEM((PHASES + 1, TOK, D), BF16), rows, rows, rows, rows, rows, columns, columns,
        pltpu.VMEM((TOK, D), BF16),
        pltpu.VMEM((TOK, D), BF16),
        pltpu.VMEM((4, TOK, HEAD), F32),
        pltpu.VMEM((TOK, HEAD), F32),
        pltpu.VMEM((TOK, HEAD), F32),
        pltpu.VMEM((PHASES, 8, HEAD), F32),
        pltpu.VMEM((PHASES, 8, HEAD), F32),
        pltpu.VMEM((2, *TILES), BF16),
        sems((PHASES,)), sems((PHASES,)), sems((PHASES,)), sems((PHASES,)), sems((1,)),
        sems((2 * GATHER_LAG, 34)), sems((2 * GATHER_LAG, 34)),
        pltpu.VMEM((2, *TILES), BF16),
        pltpu.VMEM((2, 4, 2, 4, 2, *STRIP), BF16),
        pltpu.VMEM((2, 3, 4, 4, 4, *piece), BF16),
        pltpu.VMEM((2, 3, 2, 2, 4, *piece), BF16),
        pltpu.VMEM((2, 3, 2, 4, 4, *piece), BF16),
        pltpu.VMEM((2, 3, 4, 4, *piece), BF16),
        pltpu.VMEM((2, 3, 2, 2, *piece), BF16),
        pltpu.VMEM((2, 3, 2, 4, *piece), BF16),
        pltpu.VMEM((2, 3, 4, *piece), BF16),
        pltpu.VMEM((2, 3, 3, *piece), BF16),
        pltpu.VMEM((PHASES, *STRIP), BF16),
        pltpu.VMEM((PHASES, *STRIP), BF16),
        sems((2, 34)), sems((2, 34)), sems((PHASES,)), sems((PHASES,)),
        pltpu.VMEM((PHASES, 8, HEAD), F32),
        pltpu.VMEM((WIDE_PEERS, 8, HEAD), F32),
        pltpu.VMEM((8, HEAD), F32),
        sems((PHASES,)), sems((PHASES,)), sems((WIDE_PEERS,)), sems((WIDE_PEERS,)),
        sems((2,)), sems((2,)),
    ]
    return pl.pallas_call(
        window_kernel,
        out_shape=(
            jax.ShapeDtypeStruct((PHASES, *TILES), BF16),
            jax.ShapeDtypeStruct((2, 3, 16, D), F32),
            jax.ShapeDtypeStruct((8, HEAD), F32),
        ),
        in_specs=[vmem, vmem, anywhere, vmem, anywhere, vmem, vmem, vmem],
        out_specs=[anywhere, vmem, vmem],
        scratch_shapes=scratch,
        compiler_params=pltpu.CompilerParams(
            collective_id=0, has_side_effects=True, vmem_limit_bytes=63 << 20
        ),
        name="window",
    )(
        shard, gain_rows, clips, positions, cotangent, jnp.asarray(freq),
        jnp.asarray(swap, BF16), jnp.asarray(sign),
    )


def shards(clips, positions, out_proj, qk_gains, cotangent):
    _, swap, _ = rotary_constants()
    partner = np.argmax(swap, axis=0)
    own = qk_gains[0].astype(F32)
    gain_rows = jnp.concatenate([own, own[:, partner], jnp.zeros((4, HEAD), F32)], axis=0)[None]
    _, shard, total = window(out_proj.reshape(1, 2, 3, 16, D), gain_rows, clips, positions, cotangent)
    dgain = total[0:2] + total[2:4][:, partner]
    return (shard.reshape(1, D // 16, D), dgain[None])


def solution(mesh):
    placed = (
        P(None, None, "dp", None),
        P(None, None, None, "dp"),
        P("pipe", "dp", None),
        P("pipe", None, None),
        P(None, None, "dp", None),
    )
    return jax.shard_map(
        shards,
        mesh=mesh,
        in_specs=placed,
        out_specs=(P("pipe", "dp", None), P("pipe", None, None)),
        check_vma=False,
    )
```

```python
import functools
import math

import jax
import jax.numpy as jnp
import numpy as np
from jax import lax
from jax.experimental import pallas as pl
from jax.experimental.pallas import tpu as pltpu
from jax.sharding import PartitionSpec as P

D = 1536
HEAD = 128
TOK = 128
HEADS = D // HEAD
PHASES = 8
F32 = jnp.float32
BF16 = jnp.bfloat16

NN = (((1,), (0,)), ((), ()))
NT = (((1,), (1,)), ((), ()))
TN = (((0,), (0,)), ((), ()))


def dot(a, b, dims=NN, precision=None):
    return lax.dot_general(a, b, dims, precision=precision, preferred_element_type=F32)


def rotary_constants():
    first = HEAD // 8
    rest = (HEAD - first) // 2
    freq = np.zeros((8, HEAD), np.float32)
    partner = np.zeros(HEAD, np.int32)
    sign = np.zeros((1, HEAD), np.float32)
    offset = 0
    for axis, width in enumerate((first, rest, rest)):
        half = width // 2
        values = np.float32(256.0) ** (np.float32(-2.0) * np.arange(half, dtype=np.float32) / np.float32(width))
        low = np.arange(offset, offset + half)
        high = low + half
        freq[axis, low] = values
        freq[axis, high] = values
        partner[low], partner[high] = high, low
        sign[0, low], sign[0, high] = -1.0, 1.0
        offset += width
    swap = np.zeros((HEAD, HEAD), np.float32)
    swap[partner, np.arange(HEAD)] = 1.0
    return freq, swap, sign


MESH = pl.DeviceIdType.MESH
AXES = "xyz"
GATHER_GROUP = 4
GATHER_GROUPED = 3
GATHER_START = (0, 2, 4, 6, 8, 10, 12)
GATHER_BASE = (0, 9, 15, 21, 27, 33)
ORDERS = ("xyz", "yzx", "zxy")


class Place:
    def __init__(self):
        self.pipe = lax.axis_index("pipe")
        self.dp = lax.axis_index("dp")
        self.core = self.dp % 2
        self.at = {
            "x": self.dp // 8 * 2 + self.pipe % 2,
            "y": self.pipe // 2,
            "z": self.dp // 2 % 4,
        }

    def device(self, core=None, **moved):
        c = {**self.at, **moved}
        core = self.core if core is None else core
        return (c["y"] * 2 + c["x"] % 2, (c["x"] // 2 * 4 + c["z"]) * 2 + core)

    def step(self, axis, delta):
        return (self.at[axis] + delta + 4) % 4

    def neighbour(self, axis, delta):
        return self.device(**{axis: self.step(axis, delta)})

    def sibling(self):
        return self.device(core=1 - self.core)


def greet(place):
    barrier = pltpu.get_barrier_semaphore()
    others = [place.neighbour(axis, delta) for axis in AXES for delta in (1, -1, 2)]
    others.append(place.sibling())
    others += [((place.pipe + q) % PHASES, place.dp) for q in range(1, PHASES)]
    others += [(place.pipe, (place.dp + q) % WIDE_PEERS) for q in range(1, WIDE_PEERS)]
    for other in others:
        pl.semaphore_signal(barrier, inc=1, device_id=other, device_id_type=MESH)
    pl.semaphore_wait(barrier, len(others))


WHOLE = "whole"


def half(h):
    return ("half", h)


def block(ref, lead, k, core, x, y, z):
    def plain(v):
        if v is WHOLE:
            return slice(None)
        return pl.ds(2 * v[1], 2) if isinstance(v, tuple) else v

    if x is WHOLE:
        xh, xl = slice(None), slice(None)
    elif isinstance(x, tuple):
        xh, xl = x[1], slice(None)
    else:
        xh, xl = x // 2, x % 2
    return ref.at[(*lead, plain(y), xh, plain(z), core, xl, k)]


TILES = (4, 2, 4, 2, 2, 3, 16, D // 4)


class Gather:
    def __init__(self, place, shard, gain, weights, gains, sems):
        self.place, self.shard, self.gain, self.weights, self.gains = place, shard, gain, weights, gains
        (self.first_send, self.first_recv, self.gain_send, self.gain_recv, self.own_sem, self.send, self.recv) = sems

    def piece(self, q):
        return self.shard.at[0, q % 2, :, :, pl.ds(pl.multiple_of(q // 2 * (D // 4), 128), D // 4)]

    def spot(self, owner, q):
        place = self.place
        return self.weights.at[owner, q // 2, place.dp // 8, place.dp // 2 % 4, place.core, q % 2]

    def first(self, q, owner, target):
        return pltpu.make_async_remote_copy(
            src_ref=self.piece(q), dst_ref=self.spot(owner, q),
            send_sem=self.first_send.at[q], recv_sem=self.first_recv.at[owner],
            device_id=(target, self.place.dp), device_id_type=MESH)

    def gain_copy(self, owner, q):
        return pltpu.make_async_remote_copy(
            src_ref=self.gain, dst_ref=self.gains.at[owner],
            send_sem=self.gain_send.at[q], recv_sem=self.gain_recv.at[owner],
            device_id=(q, self.place.dp), device_id_type=MESH)

    def own_copy(self):
        me = self.place.pipe
        return pltpu.make_async_copy(self.piece(me), self.spot(me, me), self.own_sem.at[0])

    def spread(self):
        me = self.place.pipe
        self.own_copy().start()
        for q in range(PHASES):
            @pl.when(q != me)
            def _():
                self.first(q, me, q).start()
                self.gain_copy(me, q).start()

            @pl.when(q == me)
            def _():
                self.gains[q] = self.gain[...]

    def arrived(self, s):
        @pl.when(s != self.place.pipe)
        def _():
            self.first(s, s, s).wait_recv()

        @pl.when(s == self.place.pipe)
        def _():
            self.own_copy().wait()

    def gains_arrived(self):
        for q in range(PHASES):
            @pl.when(q != self.place.pipe)
            def _():
                self.first(q, self.place.pipe, q).wait_send()
                self.gain_copy(self.place.pipe, q).wait_send()
                self.gain_copy(q, q).wait_recv()

    def copies(self, stage, s):
        place = self.place
        made = []

        def add(view, device):
            i = GATHER_BASE[stage] + len(made)
            made.append(pltpu.make_async_remote_copy(
                src_ref=view, dst_ref=view, send_sem=self.send.at[s, i], recv_sem=self.recv.at[s, i],
                device_id=device, device_id_type=MESH))

        if stage == 5:
            add(self.weights.at[s, :, :, :, place.core], place.sibling())
            return made
        for k, (a, b, c) in enumerate(ORDERS):
            def view(**where):
                return block(self.weights, (s,), k, place.core, **{**place.at, **where})

            if stage == 0:
                for delta in (1, -1, 2):
                    add(view(), place.neighbour(c, delta))
            elif stage == 1:
                for delta in (1, -1):
                    add(view(**{c: WHOLE}), place.neighbour(b, delta))
            elif stage == 2:
                for h, delta in enumerate((1, -1)):
                    add(view(**{b: place.step(b, -delta), c: half(h)}), place.neighbour(b, delta))
            elif stage == 3:
                for delta in (1, -1):
                    add(view(**{b: WHOLE, c: WHOLE}), place.neighbour(a, delta))
            else:
                for h, delta in enumerate((1, -1)):
                    add(view(**{a: place.step(a, -delta), b: half(h), c: WHOLE}), place.neighbour(a, delta))
        return made

    def tick(self, t):
        def move(stage, s):
            if stage:
                for copy in self.copies(stage - 1, s):
                    copy.wait()
            else:
                self.arrived(s)
            if stage < 6:
                for copy in self.copies(stage, s):
                    copy.start()

        for stage in reversed(range(7)):
            turn = t - GATHER_START[stage]
            if stage < GATHER_GROUPED:
                @pl.when((turn >= 0) & (turn < PHASES // GATHER_GROUP))
                def _():
                    def one(n, carry):
                        move(stage, turn * GATHER_GROUP + n)
                        return carry

                    lax.fori_loop(0, GATHER_GROUP, one, 0)
            else:
                @pl.when((turn >= 0) & (turn < PHASES))
                def _():
                    move(stage, turn)


STRIP = (3, 16, D // 4)
STAGE_BASE = (0, 1, 7, 13, 19, 25)
WIDE_PEERS = 16


def cut(ref, lead, k, where):
    index = []
    for axis in ORDERS[k]:
        if axis in where:
            v = where[axis]
            index.append(pl.ds(2 * v[1], 2) if isinstance(v, tuple) else v)
    return ref.at[(*lead, *index)]


def add_into(out, *parts):
    total = parts[0][...].astype(F32)
    for part in parts[1:]:
        total += part[...].astype(F32)
    out[...] = total.astype(out.dtype)


SCATTER_START = (0, 1, 3, 5, 6, 7, 8)
WIDE_SLOTS = 4


class Scatter:
    def __init__(self, place, bufs):
        self.place = place
        (self.grad, self.pair, self.wide, self.wide_half, self.wide_got, self.slim, self.slim_half,
         self.slim_got, self.last, self.last_got, self.final, self.out, self.send, self.recv,
         self.final_send, self.final_recv) = bufs

    def copies(self, stage, i):
        place, slot, broad, sem = self.place, i % 2, i % WIDE_SLOTS, i % 4
        made = []

        def add(src, dst, device):
            j = STAGE_BASE[stage] + len(made)
            made.append(pltpu.make_async_remote_copy(
                src_ref=src, dst_ref=dst, send_sem=self.send.at[sem, j], recv_sem=self.recv.at[sem, j],
                device_id=device, device_id_type=MESH))

        if stage == 0:
            add(self.grad.at[:, :, :, 1 - place.core], self.pair.at[slot], place.sibling())
            return made
        for k, (a, b, c) in enumerate(ORDERS):
            if stage == 1:
                for h, delta in enumerate((1, -1)):
                    src = cut(self.wide, (broad, k), k, {a: place.step(a, 2), b: half(h)})
                    add(src, self.wide_half.at[broad, k, h], place.neighbour(a, delta))
            elif stage == 2:
                for h, delta in enumerate((1, -1)):
                    src = cut(self.wide, (broad, k), k, {a: place.step(a, delta)})
                    add(src, self.wide_got.at[broad, k, h], place.neighbour(a, delta))
            elif stage == 3:
                for h, delta in enumerate((1, -1)):
                    src = self.slim.at[slot, k, place.step(b, 2), pl.ds(2 * h, 2)]
                    add(src, self.slim_half.at[slot, k, h], place.neighbour(b, delta))
            elif stage == 4:
                for h, delta in enumerate((1, -1)):
                    src = self.slim.at[slot, k, place.step(b, delta)]
                    add(src, self.slim_got.at[slot, k, h], place.neighbour(b, delta))
            else:
                for h, delta in enumerate((1, -1, 2)):
                    src = self.last.at[slot, k, place.step(c, delta)]
                    add(src, self.last_got.at[slot, k, h], place.neighbour(c, delta))
        return made

    def fill_wide(self, i):
        slot, broad = i % 2, i % WIDE_SLOTS
        core = self.place.core

        def row(y, carry):
            for xh in range(2):
                for xl in range(2):
                    x = xh * 2 + xl
                    for k in range(3):
                        full = slice(None)
                        where = {"x": x, "y": y, "z": full}
                        out = self.wide.at[(broad, k, *(where[axis] for axis in ORDERS[k]))]
                        add_into(out, self.grad.at[y, xh, :, core, xl, k], self.pair.at[slot, y, xh, :, xl, k])
            return carry

        lax.fori_loop(0, 4, row, 0)

    def process(self, stage, i):
        place, slot, broad = self.place, i % 2, i % WIDE_SLOTS
        if stage == 1:
            self.fill_wide(i)
            return
        for k, (a, b, c) in enumerate(ORDERS):
            if stage == 2:
                for h, delta in enumerate((1, -1)):
                    part = self.wide.at[broad, k, place.step(a, delta), pl.ds(2 * h, 2)]
                    add_into(part, part, self.wide_half.at[broad, k, h])
            elif stage == 3:
                add_into(self.slim.at[slot, k], self.wide.at[broad, k, place.at[a]],
                         self.wide_got.at[broad, k, 0], self.wide_got.at[broad, k, 1])
            elif stage == 4:
                for h, delta in enumerate((1, -1)):
                    part = self.slim.at[slot, k, place.step(b, delta), pl.ds(2 * h, 2)]
                    add_into(part, part, self.slim_half.at[slot, k, h])
            elif stage == 5:
                add_into(self.last.at[slot, k], self.slim.at[slot, k, place.at[b]],
                         self.slim_got.at[slot, k, 0], self.slim_got.at[slot, k, 1])
            else:
                add_into(self.final.at[PHASES - 1 - i, k], self.last.at[slot, k, place.at[c]],
                         *(self.last_got.at[slot, k, h] for h in range(3)))

    def final_copy(self, s, source, target):
        return pltpu.make_async_remote_copy(
            src_ref=self.final.at[s], dst_ref=self.out.at[source],
            send_sem=self.final_send.at[s], recv_sem=self.final_recv.at[source],
            device_id=(target, self.place.dp), device_id_type=MESH)

    def deliver(self, i):
        me, s = self.place.pipe, PHASES - 1 - i

        @pl.when(s != me)
        def _():
            self.final_copy(s, me, s).start()

        @pl.when(s == me)
        def _():
            self.out[s] = self.final[s]

    def settle(self):
        for q in range(PHASES):
            @pl.when(q != self.place.pipe)
            def _():
                self.final_copy(q, q, q).wait()

    def tick(self, t):
        for stage in range(6, 0, -1):
            i = t - SCATTER_START[stage]

            @pl.when((i >= 0) & (i < PHASES))
            def _():
                for copy in self.copies(stage - 1, i):
                    copy.wait()
                self.process(stage, i)
                if stage < 6:
                    for copy in self.copies(stage, i):
                        copy.start()
                else:
                    self.deliver(i)

    def begin(self, i):
        for copy in self.copies(0, i):
            copy.start()


class GainSum:
    def __init__(self, place, dgains, bufs):
        self.place, self.dgains = place, dgains
        (self.rows, self.wide, self.sum, self.send, self.recv, self.wide_send, self.wide_recv) = bufs

    def narrow(self, owner, source, target):
        return pltpu.make_async_remote_copy(
            src_ref=self.dgains.at[owner], dst_ref=self.rows.at[source],
            send_sem=self.send.at[owner], recv_sem=self.recv.at[source],
            device_id=(target, self.place.dp), device_id_type=MESH)

    def share(self, index, source, target):
        return pltpu.make_async_remote_copy(
            src_ref=self.sum, dst_ref=self.wide.at[source],
            send_sem=self.wide_send.at[index], recv_sem=self.wide_recv.at[source],
            device_id=(self.place.pipe, target), device_id_type=MESH)

    def start(self):
        me = self.place.pipe
        for q in range(PHASES):
            @pl.when(q != me)
            def _():
                self.narrow(q, me, q).start()

            @pl.when(q == me)
            def _():
                self.rows[q] = self.dgains[q]

    def middle(self):
        for q in range(PHASES):
            @pl.when(q != self.place.pipe)
            def _():
                self.narrow(q, q, q).wait()
        self.sum[...] = jnp.sum(self.rows[...], axis=0)
        for q in range(WIDE_PEERS):
            @pl.when(q != self.place.dp)
            def _():
                self.share(q, self.place.dp, q).start()

            @pl.when(q == self.place.dp)
            def _():
                self.wide[q] = self.sum[...]

    def finish(self, total, swap):
        for q in range(WIDE_PEERS):
            @pl.when(q != self.place.dp)
            def _():
                self.share(q, q, q).wait()
        rows = jnp.sum(self.wide[...], axis=0)
        moved = dot(rows, swap.astype(F32), NN, lax.Precision.HIGHEST)
        total[0] = rows[0:2] + moved[2:4]


def head(j):
    return pl.ds(j * HEAD, HEAD)


def mix_phase(s, tabs, swap, hs, qs, ks, es, ms, ns, cols):
    a0, b0, a1, b1 = tabs
    ones = jnp.ones((TOK, HEAD), BF16)
    for j in range(HEADS):
        hj = hs[s, :, head(j)]
        hf = hj.astype(F32)
        r = lax.rsqrt(jnp.mean(hf * hf, axis=-1, keepdims=True) + 1e-6)
        cols[s, :, j : j + 1] = r
        n = hf * r
        nsw = dot(hj, swap) * r
        ns[s, :, head(j)] = nsw.astype(BF16)
        qs[s, :, head(j)] = (n * a0 + nsw * b0).astype(BF16)
        ks[s, :, head(j)] = (n * a1 + nsw * b1).astype(BF16)
    for j in range(HEADS):
        scores = dot(qs[s, :, head(j)], ks[s, :, head(j)], NT)
        es[s, :, head(j)] = jnp.exp(scores).astype(BF16)
    for j in range(HEADS):
        both = dot(es[s, :, head(j)], jnp.concatenate([hs[s, :, head(j)], ones], axis=1))
        inv = 1.0 / both[:, HEAD:]
        cols[s, :, 16 + j : 17 + j] = inv[:, 0:1]
        ms[s, :, head(j)] = (both[:, :HEAD] * inv).astype(BF16)


def project_phase(s, w_ref, hs, ms):
    for c in range(4):
        cols = pl.ds(c * 384, 384)
        update = dot(ms[s], w_ref[s % 2, c].reshape(D, D // 4))
        hs[s + 1, :, cols] = (hs[s, :, cols].astype(F32) + update).astype(BF16)


def weight_phase(s, g, ms, grad_ref):
    for y in range(4):
        for t in range(4):
            part = dot(ms[s, :, pl.ds(t * 384, 384)], g[:, pl.ds(y * 384, 384)], TN).astype(BF16)
            grad_ref[y, t // 2, pl.ds(t % 2 * 2, 2)] = part.reshape(2, 2, 2, *STRIP)


def input_phase(s, w_ref, tabs, swap, g, gm, acc, hs, qs, ks, es, ms, ns, cols):
    a0, b0, a1, b1 = tabs
    for c in range(4):
        total = None
        for y in range(4):
            w = w_ref[s % 2, y, c // 2, pl.ds(c % 2 * 2, 2)].reshape(384, D // 4)
            part = dot(g[:, pl.ds(y * 384, 384)], w, NT)
            total = part if total is None else total + part
        gm[:, pl.ds(c * 384, 384)] = total.astype(BF16)
    acc[...] = jnp.zeros_like(acc)
    for j in range(HEADS):
        hj = hs[s, :, head(j)]
        ej = es[s, :, head(j)]
        qj = qs[s, :, head(j)]
        kj = ks[s, :, head(j)]
        r = cols[s, :, j : j + 1]
        gmf = gm[:, head(j)].astype(F32) * cols[s, :, 16 + j : 17 + j]
        delta = jnp.sum(gmf * ms[s, :, head(j)].astype(F32), axis=-1, keepdims=True)
        gmb = gmf.astype(BF16)
        ga = dot(gmb, hj, NT)
        ds = (ej.astype(F32) * (ga - delta)).astype(BF16)
        gv = dot(ej, gmb, TN)
        dq = dot(ds, kj)
        dk = dot(ds, qj, TN)
        n = hj.astype(F32) * r
        nsw = ns[s, :, head(j)].astype(F32)
        acc[0] += n * dq
        acc[1] += nsw * dq
        acc[2] += n * dk
        acc[3] += nsw * dk
        crossed = (dq * b0 + dk * b1).astype(BF16)
        dn = dq * a0 + dk * a1 + dot(crossed, swap, NT)
        dh = r * (dn - n * jnp.mean(dn * n, axis=-1, keepdims=True))
        g[:, head(j)] = (g[:, head(j)].astype(F32) + (dh + gv)).astype(BF16)


LIVE = 6


def window_kernel(shard_ref, gain_ref, clip_ref, pos_ref, cot_ref, freq_ref, swap_ref, sign_ref,
                  w_ref, out_ref, total_ref, *rest):
    rest = iter(rest)
    take = lambda count: [next(rest) for _ in range(count)]
    saved = take(7)
    g, gm, acc, cosine, sine, own_gains, gains, dgains, wbuf = take(9)
    gather_sems = take(7)
    scatter_bufs = take(16)
    gain_bufs = take(7)
    in_sem, w_sem = take(2)
    grad = scatter_bufs[0]
    hs = saved[0]
    place = Place()
    live = place.pipe < LIVE
    slot = jnp.minimum(place.pipe, LIVE - 1)
    clip_in = pltpu.make_async_copy(clip_ref.at[slot // 3, slot % 3], hs.at[0], in_sem.at[0])
    cot_in = pltpu.make_async_copy(cot_ref.at[slot // 3, slot % 3], g, in_sem.at[1])
    clip_in.start()
    cot_in.start()
    own_gains[...] = jnp.concatenate([gain_ref[0].astype(F32), jnp.zeros((6, HEAD), F32)], axis=0)
    greet(place)
    gather = Gather(place, shard_ref, own_gains, w_ref, gains, gather_sems)
    scatter = Scatter(place, scatter_bufs)
    sums = GainSum(place, dgains, gain_bufs)
    scale = 1.0 / math.sqrt(HEAD)
    gather.spread()
    positions = pos_ref[:, slot % 3, slot // 3, :].astype(F32)
    padded = jnp.concatenate([positions, jnp.zeros((5, TOK), F32)], axis=0)
    angles = dot(padded, freq_ref[...], TN, lax.Precision.HIGHEST)
    cosine[...] = jnp.cos(angles)
    sine[...] = jnp.sin(angles) * sign_ref[...]

    @pl.when(jnp.logical_not(live))
    def _():
        grad[...] = jnp.zeros_like(grad)
        dgains[...] = jnp.zeros_like(dgains)

    clip_in.wait()
    cot_in.wait()

    def tables(s):
        rows = gains[s]
        moved = dot(rows.astype(BF16), swap_ref[...])
        c, n = cosine[...], sine[...]
        return (c * (rows[0:1] * scale), n * (moved[0:1] * scale), c * rows[1:2], n * moved[1:2])

    def weights_in(s):
        return pltpu.make_async_copy(w_ref.at[s], wbuf.at[s % 2], w_sem.at[s % 2])

    arrive = GATHER_START[6]

    def forward_tick(t, carry):
        gather.tick(t)
        ready = t - arrive

        @pl.when(ready >= 0)
        def _():
            weights_in(ready).start()

        @pl.when(t == arrive - 3)
        def _():
            gather.gains_arrived()

            @pl.when(live)
            def _():
                mix_phase(0, tables(0), swap_ref[...], *saved)

        @pl.when(ready >= 1)
        def _():
            s = ready - 1
            weights_in(s).wait()

            @pl.when(live)
            def _():
                project_phase(s, wbuf, hs, saved[4])
                mix_phase(s + 1, tables(s + 1), swap_ref[...], *saved)

        return carry

    lax.fori_loop(0, PHASES + arrive, forward_tick, 0)

    def backward_tick(t, carry):
        scatter.tick(t)

        @pl.when(t < PHASES)
        def _():
            s = PHASES - 1 - t

            @pl.when(live)
            def _():
                weight_phase(s, g, saved[4], grad)

            scatter.begin(t)

            @pl.when(t != 1)
            def _():
                weights_in(s).wait()

            @pl.when(live)
            def _():
                input_phase(s, wbuf, tables(s), swap_ref[...], g, gm, acc, *saved)
                x0 = jnp.sum(acc[0] * cosine[...], axis=0, keepdims=True)
                y0 = jnp.sum(acc[1] * sine[...], axis=0, keepdims=True)
                x1 = jnp.sum(acc[2] * cosine[...], axis=0, keepdims=True)
                y1 = jnp.sum(acc[3] * sine[...], axis=0, keepdims=True)
                dgains[s] = jnp.concatenate([x0 * scale, x1, y0 * scale, y1, jnp.zeros((4, HEAD), F32)], axis=0)

            @pl.when(t < PHASES - 2)
            def _():
                weights_in(s - 2).start()

        @pl.when(t == PHASES)
        def _():
            sums.start()

        @pl.when(t == PHASES + 2)
        def _():
            sums.middle()

        return carry

    lax.fori_loop(0, PHASES + SCATTER_START[6], backward_tick, 0)
    sums.finish(total_ref, swap_ref[...])
    scatter.settle()
    for y in range(4):
        for xl in range(2):
            out_ref[xl, :, :, pl.ds(y * (D // 4), D // 4)] = scatter.out[y * 2 + xl].astype(F32)


def window(shard, gain_pair, clips, positions, cotangent):
    freq, swap, sign = rotary_constants()
    piece = (16, D // 4)
    sems = pltpu.SemaphoreType.DMA
    vmem = pl.BlockSpec(memory_space=pltpu.VMEM)
    anywhere = pl.BlockSpec(memory_space=pl.ANY)
    rows = pltpu.VMEM((PHASES, TOK, D), BF16)
    columns = pltpu.VMEM((PHASES, TOK, HEAD), F32)
    scratch = [
        rows, rows, rows, rows, rows, rows, columns,
        pltpu.VMEM((TOK, D), BF16),
        pltpu.VMEM((TOK, D), BF16),
        pltpu.VMEM((4, TOK, HEAD), F32),
        pltpu.VMEM((TOK, HEAD), F32),
        pltpu.VMEM((TOK, HEAD), F32),
        pltpu.VMEM((8, HEAD), F32),
        pltpu.VMEM((PHASES, 8, HEAD), F32),
        pltpu.VMEM((PHASES, 8, HEAD), F32),
        pltpu.VMEM((2, *TILES), BF16),
        sems((PHASES,)), sems((PHASES,)), sems((PHASES,)), sems((PHASES,)), sems((1,)),
        sems((PHASES, 34)), sems((PHASES, 34)),
        pltpu.VMEM(TILES, BF16),
        pltpu.VMEM((2, 4, 2, 4, 2, *STRIP), BF16),
        pltpu.VMEM((WIDE_SLOTS, 3, 4, 4, 4, *piece), BF16),
        pltpu.VMEM((WIDE_SLOTS, 3, 2, 2, 4, *piece), BF16),
        pltpu.VMEM((WIDE_SLOTS, 3, 2, 4, 4, *piece), BF16),
        pltpu.VMEM((2, 3, 4, 4, *piece), BF16),
        pltpu.VMEM((2, 3, 2, 2, *piece), BF16),
        pltpu.VMEM((2, 3, 2, 4, *piece), BF16),
        pltpu.VMEM((2, 3, 4, *piece), BF16),
        pltpu.VMEM((2, 3, 3, *piece), BF16),
        pltpu.VMEM((PHASES, *STRIP), BF16),
        pltpu.VMEM((PHASES, *STRIP), BF16),
        sems((4, 34)), sems((4, 34)), sems((PHASES,)), sems((PHASES,)),
        pltpu.VMEM((PHASES, 8, HEAD), F32),
        pltpu.VMEM((WIDE_PEERS, 8, HEAD), F32),
        pltpu.VMEM((8, HEAD), F32),
        sems((PHASES,)), sems((PHASES,)), sems((WIDE_PEERS,)), sems((WIDE_PEERS,)),
        sems((2,)), sems((2,)),
    ]
    return pl.pallas_call(
        window_kernel,
        out_shape=(
            jax.ShapeDtypeStruct((PHASES, *TILES), BF16),
            jax.ShapeDtypeStruct((2, 3, 16, D), F32),
            jax.ShapeDtypeStruct((1, 2, HEAD), F32),
        ),
        in_specs=[vmem, vmem, anywhere, vmem, anywhere, vmem, vmem, vmem],
        out_specs=[anywhere, vmem, vmem],
        scratch_shapes=scratch,
        compiler_params=pltpu.CompilerParams(
            collective_id=0, has_side_effects=True, vmem_limit_bytes=63 << 20
        ),
        name="window",
    )(
        shard, gain_pair, clips, positions.transpose(0, 2, 1, 3), cotangent, jnp.asarray(freq),
        jnp.asarray(swap, BF16), jnp.asarray(sign),
    )


def shards(clips, positions, out_proj, qk_gains, cotangent):
    _, shard, dgain = window(out_proj.reshape(1, 2, 3, 16, D), qk_gains, clips, positions, cotangent)
    return (shard.reshape(1, D // 16, D), dgain)


def solution(mesh):
    placed = (
        P(None, None, "dp", None),
        P(None, None, None, "dp"),
        P("pipe", "dp", None),
        P("pipe", None, None),
        P(None, None, "dp", None),
    )
    return jax.shard_map(
        shards,
        mesh=mesh,
        in_specs=placed,
        out_specs=(P("pipe", "dp", None), P("pipe", None, None)),
        check_vma=False,
    )
```

```python
import functools
import math

import jax
import jax.numpy as jnp
import numpy as np
from jax import lax
from jax.experimental import pallas as pl
from jax.experimental.pallas import tpu as pltpu
from jax.sharding import PartitionSpec as P

D = 1536
HEAD = 128
TOK = 128
HEADS = D // HEAD
PHASES = 8
F32 = jnp.float32
BF16 = jnp.bfloat16

NN = (((1,), (0,)), ((), ()))
NT = (((1,), (1,)), ((), ()))
TN = (((0,), (0,)), ((), ()))


def dot(a, b, dims=NN, precision=None):
    return lax.dot_general(a, b, dims, precision=precision, preferred_element_type=F32)


def rotary_constants():
    first = HEAD // 8
    rest = (HEAD - first) // 2
    freq = np.zeros((8, HEAD), np.float32)
    partner = np.zeros(HEAD, np.int32)
    sign = np.zeros((1, HEAD), np.float32)
    offset = 0
    for axis, width in enumerate((first, rest, rest)):
        half = width // 2
        values = np.float32(256.0) ** (np.float32(-2.0) * np.arange(half, dtype=np.float32) / np.float32(width))
        low = np.arange(offset, offset + half)
        high = low + half
        freq[axis, low] = values
        freq[axis, high] = values
        partner[low], partner[high] = high, low
        sign[0, low], sign[0, high] = -1.0, 1.0
        offset += width
    swap = np.zeros((HEAD, HEAD), np.float32)
    swap[partner, np.arange(HEAD)] = 1.0
    return freq, swap, sign


MESH = pl.DeviceIdType.MESH
AXES = "xyz"
GATHER_GROUP = 4
GATHER_GROUPED = 3
GATHER_START = (0, 2, 4, 6, 8, 10, 12)
GATHER_BASE = (0, 9, 15, 21, 27, 33)
ORDERS = ("xyz", "yzx", "zxy")


class Place:
    def __init__(self):
        self.pipe = lax.axis_index("pipe")
        self.dp = lax.axis_index("dp")
        self.core = self.dp % 2
        self.at = {
            "x": self.dp // 8 * 2 + self.pipe % 2,
            "y": self.pipe // 2,
            "z": self.dp // 2 % 4,
        }

    def device(self, core=None, **moved):
        c = {**self.at, **moved}
        core = self.core if core is None else core
        return (c["y"] * 2 + c["x"] % 2, (c["x"] // 2 * 4 + c["z"]) * 2 + core)

    def step(self, axis, delta):
        return (self.at[axis] + delta + 4) % 4

    def neighbour(self, axis, delta):
        return self.device(**{axis: self.step(axis, delta)})

    def sibling(self):
        return self.device(core=1 - self.core)


def greet(place):
    barrier = pltpu.get_barrier_semaphore()
    others = [place.neighbour(axis, delta) for axis in AXES for delta in (1, -1, 2)]
    others.append(place.sibling())
    others += [((place.pipe + q) % PHASES, place.dp) for q in range(1, PHASES)]
    others += [(place.pipe, (place.dp + q) % WIDE_PEERS) for q in range(1, WIDE_PEERS)]
    for other in others:
        pl.semaphore_signal(barrier, inc=1, device_id=other, device_id_type=MESH)
    pl.semaphore_wait(barrier, len(others))


WHOLE = "whole"


def half(h):
    return ("half", h)


def block(ref, lead, k, core, x, y, z):
    def plain(v):
        if v is WHOLE:
            return slice(None)
        return pl.ds(2 * v[1], 2) if isinstance(v, tuple) else v

    if x is WHOLE:
        xh, xl = slice(None), slice(None)
    elif isinstance(x, tuple):
        xh, xl = x[1], slice(None)
    else:
        xh, xl = x // 2, x % 2
    return ref.at[(*lead, plain(y), xh, plain(z), core, xl, k)]


TILES = (4, 2, 4, 2, 2, 3, 16, D // 4)


class Gather:
    def __init__(self, place, shard, gain, weights, gains, sems):
        self.place, self.shard, self.gain, self.weights, self.gains = place, shard, gain, weights, gains
        (self.first_send, self.first_recv, self.gain_send, self.gain_recv, self.own_sem, self.send, self.recv) = sems

    def piece(self, q):
        return self.shard.at[0, q % 2, :, :, pl.ds(pl.multiple_of(q // 2 * (D // 4), 128), D // 4)]

    def spot(self, owner, q):
        place = self.place
        return self.weights.at[owner, q // 2, place.dp // 8, place.dp // 2 % 4, place.core, q % 2]

    def first(self, q, owner, target):
        return pltpu.make_async_remote_copy(
            src_ref=self.piece(q), dst_ref=self.spot(owner, q),
            send_sem=self.first_send.at[q], recv_sem=self.first_recv.at[owner],
            device_id=(target, self.place.dp), device_id_type=MESH)

    def gain_copy(self, owner, q):
        return pltpu.make_async_remote_copy(
            src_ref=self.gain, dst_ref=self.gains.at[owner],
            send_sem=self.gain_send.at[q], recv_sem=self.gain_recv.at[owner],
            device_id=(q, self.place.dp), device_id_type=MESH)

    def own_copy(self):
        me = self.place.pipe
        return pltpu.make_async_copy(self.piece(me), self.spot(me, me), self.own_sem.at[0])

    def spread(self):
        me = self.place.pipe
        self.own_copy().start()
        for q in range(PHASES):
            @pl.when(q != me)
            def _():
                self.first(q, me, q).start()
                self.gain_copy(me, q).start()

            @pl.when(q == me)
            def _():
                self.gains[q] = self.gain[...]

    def arrived(self, s):
        @pl.when(s != self.place.pipe)
        def _():
            self.first(s, s, s).wait_recv()

        @pl.when(s == self.place.pipe)
        def _():
            self.own_copy().wait()

    def gains_arrived(self):
        for q in range(PHASES):
            @pl.when(q != self.place.pipe)
            def _():
                self.first(q, self.place.pipe, q).wait_send()
                self.gain_copy(self.place.pipe, q).wait_send()
                self.gain_copy(q, q).wait_recv()

    def copies(self, stage, s):
        place = self.place
        made = []

        def add(view, device):
            i = GATHER_BASE[stage] + len(made)
            made.append(pltpu.make_async_remote_copy(
                src_ref=view, dst_ref=view, send_sem=self.send.at[s, i], recv_sem=self.recv.at[s, i],
                device_id=device, device_id_type=MESH))

        if stage == 5:
            add(self.weights.at[s, :, :, :, place.core], place.sibling())
            return made
        for k, (a, b, c) in enumerate(ORDERS):
            def view(**where):
                return block(self.weights, (s,), k, place.core, **{**place.at, **where})

            if stage == 0:
                for delta in (1, -1, 2):
                    add(view(), place.neighbour(c, delta))
            elif stage == 1:
                for delta in (1, -1):
                    add(view(**{c: WHOLE}), place.neighbour(b, delta))
            elif stage == 2:
                for h, delta in enumerate((1, -1)):
                    add(view(**{b: place.step(b, -delta), c: half(h)}), place.neighbour(b, delta))
            elif stage == 3:
                for delta in (1, -1):
                    add(view(**{b: WHOLE, c: WHOLE}), place.neighbour(a, delta))
            else:
                for h, delta in enumerate((1, -1)):
                    add(view(**{a: place.step(a, -delta), b: half(h), c: WHOLE}), place.neighbour(a, delta))
        return made

    def tick(self, t):
        def move(stage, s):
            if stage:
                for copy in self.copies(stage - 1, s):
                    copy.wait()
            else:
                self.arrived(s)
            if stage < 6:
                for copy in self.copies(stage, s):
                    copy.start()

        for stage in reversed(range(7)):
            turn = t - GATHER_START[stage]
            if stage < GATHER_GROUPED:
                @pl.when((turn >= 0) & (turn < PHASES // GATHER_GROUP))
                def _():
                    def one(n, carry):
                        move(stage, turn * GATHER_GROUP + n)
                        return carry

                    lax.fori_loop(0, GATHER_GROUP, one, 0)
            else:
                @pl.when((turn >= 0) & (turn < PHASES))
                def _():
                    move(stage, turn)


STRIP = (3, 16, D // 4)
STAGE_BASE = (0, 1, 7, 13, 19, 25)
WIDE_PEERS = 16


def cut(ref, lead, k, where):
    index = []
    for axis in ORDERS[k]:
        if axis in where:
            v = where[axis]
            index.append(pl.ds(2 * v[1], 2) if isinstance(v, tuple) else v)
    return ref.at[(*lead, *index)]


def add_into(out, *parts):
    if len(parts) == 2:
        out[...] = parts[0][...] + parts[1][...]
        return
    total = parts[0][...].astype(F32)
    for part in parts[1:]:
        total += part[...].astype(F32)
    out[...] = total.astype(out.dtype)


SCATTER_START = (0, 1, 3, 5, 6, 7, 8)
WIDE_SLOTS = 4


class Scatter:
    def __init__(self, place, bufs):
        self.place = place
        (self.grad, self.pair, self.wide, self.wide_half, self.wide_got, self.slim, self.slim_half,
         self.slim_got, self.last, self.last_got, self.final, self.out, self.send, self.recv,
         self.final_send, self.final_recv) = bufs

    def copies(self, stage, i):
        place, slot, broad, sem = self.place, i % 2, i % WIDE_SLOTS, i % 4
        made = []

        def add(src, dst, device):
            j = STAGE_BASE[stage] + len(made)
            made.append(pltpu.make_async_remote_copy(
                src_ref=src, dst_ref=dst, send_sem=self.send.at[sem, j], recv_sem=self.recv.at[sem, j],
                device_id=device, device_id_type=MESH))

        if stage == 0:
            add(self.grad.at[:, :, :, 1 - place.core], self.pair.at[slot], place.sibling())
            return made
        for k, (a, b, c) in enumerate(ORDERS):
            if stage == 1:
                for h, delta in enumerate((1, -1)):
                    src = cut(self.wide, (broad, k), k, {a: place.step(a, 2), b: half(h)})
                    add(src, self.wide_half.at[broad, k, h], place.neighbour(a, delta))
            elif stage == 2:
                for h, delta in enumerate((1, -1)):
                    src = cut(self.wide, (broad, k), k, {a: place.step(a, delta)})
                    add(src, self.wide_got.at[broad, k, h], place.neighbour(a, delta))
            elif stage == 3:
                for h, delta in enumerate((1, -1)):
                    src = self.slim.at[slot, k, place.step(b, 2), pl.ds(2 * h, 2)]
                    add(src, self.slim_half.at[slot, k, h], place.neighbour(b, delta))
            elif stage == 4:
                for h, delta in enumerate((1, -1)):
                    src = self.slim.at[slot, k, place.step(b, delta)]
                    add(src, self.slim_got.at[slot, k, h], place.neighbour(b, delta))
            else:
                for h, delta in enumerate((1, -1, 2)):
                    src = self.last.at[slot, k, place.step(c, delta)]
                    add(src, self.last_got.at[slot, k, h], place.neighbour(c, delta))
        return made

    def fill_wide(self, i):
        slot, broad = i % 2, i % WIDE_SLOTS
        core = self.place.core

        def row(y, carry):
            for xh in range(2):
                for xl in range(2):
                    x = xh * 2 + xl
                    for k in range(3):
                        full = slice(None)
                        where = {"x": x, "y": y, "z": full}
                        out = self.wide.at[(broad, k, *(where[axis] for axis in ORDERS[k]))]
                        add_into(out, self.grad.at[y, xh, :, core, xl, k], self.pair.at[slot, y, xh, :, xl, k])
            return carry

        lax.fori_loop(0, 4, row, 0)

    def process(self, stage, i):
        place, slot, broad = self.place, i % 2, i % WIDE_SLOTS
        if stage == 1:
            self.fill_wide(i)
            return
        for k, (a, b, c) in enumerate(ORDERS):
            if stage == 2:
                for h, delta in enumerate((1, -1)):
                    part = self.wide.at[broad, k, place.step(a, delta), pl.ds(2 * h, 2)]
                    add_into(part, part, self.wide_half.at[broad, k, h])
            elif stage == 3:
                add_into(self.slim.at[slot, k], self.wide.at[broad, k, place.at[a]],
                         self.wide_got.at[broad, k, 0], self.wide_got.at[broad, k, 1])
            elif stage == 4:
                for h, delta in enumerate((1, -1)):
                    part = self.slim.at[slot, k, place.step(b, delta), pl.ds(2 * h, 2)]
                    add_into(part, part, self.slim_half.at[slot, k, h])
            elif stage == 5:
                add_into(self.last.at[slot, k], self.slim.at[slot, k, place.at[b]],
                         self.slim_got.at[slot, k, 0], self.slim_got.at[slot, k, 1])
            else:
                add_into(self.final.at[PHASES - 1 - i, k], self.last.at[slot, k, place.at[c]],
                         *(self.last_got.at[slot, k, h] for h in range(3)))

    def final_copy(self, s, source, target):
        return pltpu.make_async_remote_copy(
            src_ref=self.final.at[s], dst_ref=self.out.at[source],
            send_sem=self.final_send.at[s], recv_sem=self.final_recv.at[source],
            device_id=(target, self.place.dp), device_id_type=MESH)

    def deliver(self, i):
        me, s = self.place.pipe, PHASES - 1 - i

        @pl.when(s != me)
        def _():
            self.final_copy(s, me, s).start()

        @pl.when(s == me)
        def _():
            self.out[s] = self.final[s]

    def settle(self):
        for q in range(PHASES):
            @pl.when(q != self.place.pipe)
            def _():
                self.final_copy(q, q, q).wait()

    def tick(self, t):
        for stage in range(6, 0, -1):
            i = t - SCATTER_START[stage]

            @pl.when((i >= 0) & (i < PHASES))
            def _():
                for copy in self.copies(stage - 1, i):
                    copy.wait()
                self.process(stage, i)
                if stage < 6:
                    for copy in self.copies(stage, i):
                        copy.start()
                else:
                    self.deliver(i)

    def begin(self, i):
        for copy in self.copies(0, i):
            copy.start()


class GainSum:
    def __init__(self, place, dgains, bufs):
        self.place, self.dgains = place, dgains
        (self.rows, self.wide, self.sum, self.send, self.recv, self.wide_send, self.wide_recv) = bufs

    def narrow(self, owner, source, target):
        return pltpu.make_async_remote_copy(
            src_ref=self.dgains.at[owner], dst_ref=self.rows.at[source],
            send_sem=self.send.at[owner], recv_sem=self.recv.at[source],
            device_id=(target, self.place.dp), device_id_type=MESH)

    def share(self, index, source, target):
        return pltpu.make_async_remote_copy(
            src_ref=self.sum, dst_ref=self.wide.at[source],
            send_sem=self.wide_send.at[index], recv_sem=self.wide_recv.at[source],
            device_id=(self.place.pipe, target), device_id_type=MESH)

    def start(self):
        me = self.place.pipe
        for q in range(PHASES):
            @pl.when(q != me)
            def _():
                self.narrow(q, me, q).start()

            @pl.when(q == me)
            def _():
                self.rows[q] = self.dgains[q]

    def middle(self):
        for q in range(PHASES):
            @pl.when(q != self.place.pipe)
            def _():
                self.narrow(q, q, q).wait()
        self.sum[...] = jnp.sum(self.rows[...], axis=0)
        for q in range(WIDE_PEERS):
            @pl.when(q != self.place.dp)
            def _():
                self.share(q, self.place.dp, q).start()

            @pl.when(q == self.place.dp)
            def _():
                self.wide[q] = self.sum[...]

    def finish(self, total, swap):
        for q in range(WIDE_PEERS):
            @pl.when(q != self.place.dp)
            def _():
                self.share(q, q, q).wait()
        rows = jnp.sum(self.wide[...], axis=0)
        moved = dot(rows, swap.astype(F32), NN, lax.Precision.HIGHEST)
        total[0] = rows[0:2] + moved[2:4]


def head(j):
    return pl.ds(j * HEAD, HEAD)


def mix_phase(s, tabs, swap, hs, qs, ks, es, ms, ns, cols):
    a0, b0, a1, b1 = tabs
    ones = jnp.ones((TOK, HEAD), BF16)
    for j in range(HEADS):
        hj = hs[s, :, head(j)]
        hf = hj.astype(F32)
        r = lax.rsqrt(jnp.mean(hf * hf, axis=-1, keepdims=True) + 1e-6)
        cols[s, :, j : j + 1] = r
        n = hf * r
        nsw = dot(hj, swap) * r
        ns[s, :, head(j)] = nsw.astype(BF16)
        qs[s, :, head(j)] = (n * a0 + nsw * b0).astype(BF16)
        ks[s, :, head(j)] = (n * a1 + nsw * b1).astype(BF16)
    for j in range(HEADS):
        scores = dot(qs[s, :, head(j)], ks[s, :, head(j)], NT)
        es[s, :, head(j)] = jnp.exp(scores).astype(BF16)
    for j in range(HEADS):
        both = dot(es[s, :, head(j)], jnp.concatenate([hs[s, :, head(j)], ones], axis=1))
        inv = 1.0 / both[:, HEAD:]
        cols[s, :, 16 + j : 17 + j] = inv[:, 0:1]
        ms[s, :, head(j)] = (both[:, :HEAD] * inv).astype(BF16)


def project_phase(s, w_ref, hs, ms):
    for c in range(4):
        cols = pl.ds(c * 384, 384)
        update = dot(ms[s], w_ref[s % 2, c].reshape(D, D // 4))
        hs[s + 1, :, cols] = (hs[s, :, cols].astype(F32) + update).astype(BF16)


def weight_phase(s, g, ms, grad_ref):
    for y in range(4):
        for t in range(4):
            part = dot(ms[s, :, pl.ds(t * 384, 384)], g[:, pl.ds(y * 384, 384)], TN).astype(BF16)
            grad_ref[y, t // 2, pl.ds(t % 2 * 2, 2)] = part.reshape(2, 2, 2, *STRIP)


def input_phase(s, w_ref, tabs, swap, g, gm, dsc, cosine, sine, hs, qs, ks, es, ms, ns, cols):
    a0, b0, a1, b1 = tabs
    for c in range(4):
        total = None
        for y in range(4):
            w = w_ref[s % 2, y, c // 2, pl.ds(c % 2 * 2, 2)].reshape(384, D // 4)
            part = dot(g[:, pl.ds(y * 384, 384)], w, NT)
            total = part if total is None else total + part
        gm[:, pl.ds(c * 384, 384)] = total.astype(BF16)
    for j in range(HEADS):
        gmf = gm[:, head(j)].astype(F32) * cols[s, :, 16 + j : 17 + j]
        gmb = gmf.astype(BF16)
        delta = jnp.sum(gmf * ms[s, :, head(j)].astype(F32), axis=-1, keepdims=True)
        ga = dot(gmb, hs[s, :, head(j)], NT)
        dsc[:, head(j)] = (es[s, :, head(j)].astype(F32) * (ga - delta)).astype(BF16)
        gm[:, head(j)] = gmb
    sums = [jnp.zeros((8, HEAD), F32)] * 4

    def folded(total, value):
        return total + jnp.sum(value.reshape(TOK // 8, 8, HEAD), axis=0)

    for j in range(HEADS):
        hj = hs[s, :, head(j)]
        r = cols[s, :, j : j + 1]
        ds = dsc[:, head(j)]
        dq = dot(ds, ks[s, :, head(j)])
        dk = dot(ds, qs[s, :, head(j)], TN)
        n = hj.astype(F32) * r
        nsw = ns[s, :, head(j)].astype(F32)
        c, sn = cosine[...], sine[...]
        nc, sc = n * c, nsw * sn
        sums = [folded(t, v) for t, v in zip(sums, (nc * dq, sc * dq, nc * dk, sc * dk))]
        crossed = (dq * b0 + dk * b1).astype(BF16)
        dn = dq * a0 + dk * a1 + dot(crossed, swap, NT)
        dh = r * (dn - n * jnp.mean(dn * n, axis=-1, keepdims=True))
        gv = dot(es[s, :, head(j)], gm[:, head(j)], TN)
        g[:, head(j)] = (g[:, head(j)].astype(F32) + (dh + gv)).astype(BF16)
    return [jnp.sum(t, axis=0, keepdims=True) for t in sums]


LIVE = 6


def window_kernel(shard_ref, gain_ref, clip_ref, pos_ref, cot_ref, freq_ref, swap_ref, sign_ref,
                  w_ref, out_ref, total_ref, *rest):
    rest = iter(rest)
    take = lambda count: [next(rest) for _ in range(count)]
    saved = take(7)
    g, gm, dsc, cosine, sine, own_gains, gains, dgains, wbuf = take(9)
    gather_sems = take(7)
    scatter_bufs = take(16)
    gain_bufs = take(7)
    in_sem, w_sem = take(2)
    grad = scatter_bufs[0]
    hs = saved[0]
    place = Place()
    live = place.pipe < LIVE
    slot = jnp.minimum(place.pipe, LIVE - 1)
    clip_in = pltpu.make_async_copy(clip_ref.at[slot // 3, slot % 3], hs.at[0], in_sem.at[0])
    cot_in = pltpu.make_async_copy(cot_ref.at[slot // 3, slot % 3], g, in_sem.at[1])
    clip_in.start()
    cot_in.start()
    own_gains[...] = jnp.concatenate([gain_ref[0].astype(F32), jnp.zeros((6, HEAD), F32)], axis=0)
    greet(place)
    gather = Gather(place, shard_ref, own_gains, w_ref, gains, gather_sems)
    scatter = Scatter(place, scatter_bufs)
    sums = GainSum(place, dgains, gain_bufs)
    scale = 1.0 / math.sqrt(HEAD)
    gather.spread()
    positions = pos_ref[:, slot % 3, slot // 3, :].astype(F32)
    padded = jnp.concatenate([positions, jnp.zeros((5, TOK), F32)], axis=0)
    angles = dot(padded, freq_ref[...], TN, lax.Precision.HIGHEST)
    cosine[...] = jnp.cos(angles)
    sine[...] = jnp.sin(angles) * sign_ref[...]

    @pl.when(jnp.logical_not(live))
    def _():
        grad[...] = jnp.zeros_like(grad)
        dgains[...] = jnp.zeros_like(dgains)

    clip_in.wait()
    cot_in.wait()

    def tables(s):
        rows = gains[s]
        moved = dot(rows.astype(BF16), swap_ref[...])
        c, n = cosine[...], sine[...]
        return (c * (rows[0:1] * scale), n * (moved[0:1] * scale), c * rows[1:2], n * moved[1:2])

    def weights_in(s):
        return pltpu.make_async_copy(w_ref.at[s], wbuf.at[s % 2], w_sem.at[s % 2])

    arrive = GATHER_START[6]

    def forward_tick(t, carry):
        gather.tick(t)
        ready = t - arrive

        @pl.when(ready >= 0)
        def _():
            weights_in(ready).start()

        @pl.when(t == arrive - 3)
        def _():
            gather.gains_arrived()

            @pl.when(live)
            def _():
                mix_phase(0, tables(0), swap_ref[...], *saved)

        @pl.when(ready >= 1)
        def _():
            s = ready - 1
            weights_in(s).wait()

            @pl.when(live)
            def _():
                project_phase(s, wbuf, hs, saved[4])
                mix_phase(s + 1, tables(s + 1), swap_ref[...], *saved)

        return carry

    lax.fori_loop(0, PHASES + arrive, forward_tick, 0)

    def backward_tick(t, carry):
        scatter.tick(t)

        @pl.when(t < PHASES)
        def _():
            s = PHASES - 1 - t

            @pl.when(live)
            def _():
                weight_phase(s, g, saved[4], grad)

            scatter.begin(t)

            @pl.when(t != 1)
            def _():
                weights_in(s).wait()

            @pl.when(live)
            def _():
                x0, y0, x1, y1 = input_phase(s, wbuf, tables(s), swap_ref[...], g, gm, dsc, cosine, sine, *saved)
                dgains[s] = jnp.concatenate([x0 * scale, x1, y0 * scale, y1, jnp.zeros((4, HEAD), F32)], axis=0)

            @pl.when(t < PHASES - 2)
            def _():
                weights_in(s - 2).start()

        @pl.when(t == PHASES)
        def _():
            sums.start()

        @pl.when(t == PHASES + 2)
        def _():
            sums.middle()

        return carry

    lax.fori_loop(0, PHASES + SCATTER_START[6], backward_tick, 0)
    sums.finish(total_ref, swap_ref[...])
    scatter.settle()
    for y in range(4):
        for xl in range(2):
            out_ref[xl, :, :, pl.ds(y * (D // 4), D // 4)] = scatter.out[y * 2 + xl].astype(F32)


def window(shard, gain_pair, clips, positions, cotangent):
    freq, swap, sign = rotary_constants()
    piece = (16, D // 4)
    sems = pltpu.SemaphoreType.DMA
    vmem = pl.BlockSpec(memory_space=pltpu.VMEM)
    anywhere = pl.BlockSpec(memory_space=pl.ANY)
    rows = pltpu.VMEM((PHASES, TOK, D), BF16)
    columns = pltpu.VMEM((PHASES, TOK, HEAD), F32)
    scratch = [
        rows, rows, rows, rows, rows, rows, columns,
        pltpu.VMEM((TOK, D), BF16),
        pltpu.VMEM((TOK, D), BF16),
        pltpu.VMEM((TOK, D), BF16),
        pltpu.VMEM((TOK, HEAD), F32),
        pltpu.VMEM((TOK, HEAD), F32),
        pltpu.VMEM((8, HEAD), F32),
        pltpu.VMEM((PHASES, 8, HEAD), F32),
        pltpu.VMEM((PHASES, 8, HEAD), F32),
        pltpu.VMEM((2, *TILES), BF16),
        sems((PHASES,)), sems((PHASES,)), sems((PHASES,)), sems((PHASES,)), sems((1,)),
        sems((PHASES, 34)), sems((PHASES, 34)),
        pltpu.VMEM(TILES, BF16),
        pltpu.VMEM((2, 4, 2, 4, 2, *STRIP), BF16),
        pltpu.VMEM((WIDE_SLOTS, 3, 4, 4, 4, *piece), BF16),
        pltpu.VMEM((WIDE_SLOTS, 3, 2, 2, 4, *piece), BF16),
        pltpu.VMEM((WIDE_SLOTS, 3, 2, 4, 4, *piece), BF16),
        pltpu.VMEM((2, 3, 4, 4, *piece), BF16),
        pltpu.VMEM((2, 3, 2, 2, *piece), BF16),
        pltpu.VMEM((2, 3, 2, 4, *piece), BF16),
        pltpu.VMEM((2, 3, 4, *piece), BF16),
        pltpu.VMEM((2, 3, 3, *piece), BF16),
        pltpu.VMEM((PHASES, *STRIP), BF16),
        pltpu.VMEM((PHASES, *STRIP), BF16),
        sems((4, 34)), sems((4, 34)), sems((PHASES,)), sems((PHASES,)),
        pltpu.VMEM((PHASES, 8, HEAD), F32),
        pltpu.VMEM((WIDE_PEERS, 8, HEAD), F32),
        pltpu.VMEM((8, HEAD), F32),
        sems((PHASES,)), sems((PHASES,)), sems((WIDE_PEERS,)), sems((WIDE_PEERS,)),
        sems((2,)), sems((2,)),
    ]
    return pl.pallas_call(
        window_kernel,
        out_shape=(
            jax.ShapeDtypeStruct((PHASES, *TILES), BF16),
            jax.ShapeDtypeStruct((2, 3, 16, D), F32),
            jax.ShapeDtypeStruct((1, 2, HEAD), F32),
        ),
        in_specs=[vmem, vmem, anywhere, vmem, anywhere, vmem, vmem, vmem],
        out_specs=[anywhere, vmem, vmem],
        scratch_shapes=scratch,
        compiler_params=pltpu.CompilerParams(
            collective_id=0, has_side_effects=True, vmem_limit_bytes=63 << 20
        ),
        name="window",
    )(
        shard, gain_pair, clips, positions.transpose(0, 2, 1, 3), cotangent, jnp.asarray(freq),
        jnp.asarray(swap, BF16), jnp.asarray(sign),
    )


def shards(clips, positions, out_proj, qk_gains, cotangent):
    _, shard, dgain = window(out_proj.reshape(1, 2, 3, 16, D), qk_gains, clips, positions, cotangent)
    return (shard.reshape(1, D // 16, D), dgain)


def solution(mesh):
    placed = (
        P(None, None, "dp", None),
        P(None, None, None, "dp"),
        P("pipe", "dp", None),
        P("pipe", None, None),
        P(None, None, "dp", None),
    )
    return jax.shard_map(
        shards,
        mesh=mesh,
        in_specs=placed,
        out_specs=(P("pipe", "dp", None), P("pipe", None, None)),
        check_vma=False,
    )
```

```python
import functools
import math

import jax
import jax.numpy as jnp
import numpy as np
from jax import lax
from jax.experimental import pallas as pl
from jax.experimental.pallas import tpu as pltpu
from jax.sharding import PartitionSpec as P

D = 1536
HEAD = 128
TOK = 128
HEADS = D // HEAD
PHASES = 8
F32 = jnp.float32
BF16 = jnp.bfloat16

NN = (((1,), (0,)), ((), ()))
NT = (((1,), (1,)), ((), ()))
TN = (((0,), (0,)), ((), ()))


def dot(a, b, dims=NN, precision=None):
    return lax.dot_general(a, b, dims, precision=precision, preferred_element_type=F32)


def rotary_constants():
    first = HEAD // 8
    rest = (HEAD - first) // 2
    freq = np.zeros((8, HEAD), np.float32)
    partner = np.zeros(HEAD, np.int32)
    sign = np.zeros((1, HEAD), np.float32)
    offset = 0
    for axis, width in enumerate((first, rest, rest)):
        half = width // 2
        values = np.float32(256.0) ** (np.float32(-2.0) * np.arange(half, dtype=np.float32) / np.float32(width))
        low = np.arange(offset, offset + half)
        high = low + half
        freq[axis, low] = values
        freq[axis, high] = values
        partner[low], partner[high] = high, low
        sign[0, low], sign[0, high] = -1.0, 1.0
        offset += width
    swap = np.zeros((HEAD, HEAD), np.float32)
    swap[partner, np.arange(HEAD)] = 1.0
    return freq, swap, sign


MESH = pl.DeviceIdType.MESH
AXES = "xyz"
GATHER_GROUP = 4
GATHER_GROUPED = 3
GATHER_START = (0, 2, 4, 6, 8, 10, 12)
GATHER_BASE = (0, 9, 15, 21, 27, 33)
ORDERS = ("xyz", "yzx", "zxy")


class Place:
    def __init__(self):
        self.pipe = lax.axis_index("pipe")
        self.dp = lax.axis_index("dp")
        self.core = self.dp % 2
        self.at = {
            "x": self.dp // 8 * 2 + self.pipe % 2,
            "y": self.pipe // 2,
            "z": self.dp // 2 % 4,
        }

    def device(self, core=None, **moved):
        c = {**self.at, **moved}
        core = self.core if core is None else core
        return (c["y"] * 2 + c["x"] % 2, (c["x"] // 2 * 4 + c["z"]) * 2 + core)

    def step(self, axis, delta):
        return (self.at[axis] + delta + 4) % 4

    def neighbour(self, axis, delta):
        return self.device(**{axis: self.step(axis, delta)})

    def sibling(self):
        return self.device(core=1 - self.core)


def greet(place):
    barrier = pltpu.get_barrier_semaphore()
    others = [place.neighbour(axis, delta) for axis in AXES for delta in (1, -1, 2)]
    others.append(place.sibling())
    others += [((place.pipe + q) % PHASES, place.dp) for q in range(1, PHASES)]
    others += [(place.pipe, (place.dp + q) % WIDE_PEERS) for q in range(1, WIDE_PEERS)]
    for other in others:
        pl.semaphore_signal(barrier, inc=1, device_id=other, device_id_type=MESH)
    pl.semaphore_wait(barrier, len(others))


WHOLE = "whole"


def half(h):
    return ("half", h)


def block(ref, lead, k, core, x, y, z):
    def plain(v):
        if v is WHOLE:
            return slice(None)
        return pl.ds(2 * v[1], 2) if isinstance(v, tuple) else v

    if x is WHOLE:
        xh, xl = slice(None), slice(None)
    elif isinstance(x, tuple):
        xh, xl = x[1], slice(None)
    else:
        xh, xl = x // 2, x % 2
    return ref.at[(*lead, plain(y), xh, plain(z), core, xl, k)]


TILES = (4, 2, 4, 2, 2, 3, 16, D // 4)


class Gather:
    def __init__(self, place, shard, gain, weights, gains, sems):
        self.place, self.shard, self.gain, self.weights, self.gains = place, shard, gain, weights, gains
        (self.first_send, self.first_recv, self.gain_send, self.gain_recv, self.own_sem, self.send, self.recv) = sems

    def piece(self, q):
        return self.shard.at[0, q % 2, :, :, pl.ds(pl.multiple_of(q // 2 * (D // 4), 128), D // 4)]

    def spot(self, owner, q):
        place = self.place
        return self.weights.at[owner, q // 2, place.dp // 8, place.dp // 2 % 4, place.core, q % 2]

    def first(self, q, owner, target):
        return pltpu.make_async_remote_copy(
            src_ref=self.piece(q), dst_ref=self.spot(owner, q),
            send_sem=self.first_send.at[q], recv_sem=self.first_recv.at[owner],
            device_id=(target, self.place.dp), device_id_type=MESH)

    def gain_copy(self, owner, q):
        return pltpu.make_async_remote_copy(
            src_ref=self.gain, dst_ref=self.gains.at[owner],
            send_sem=self.gain_send.at[q], recv_sem=self.gain_recv.at[owner],
            device_id=(q, self.place.dp), device_id_type=MESH)

    def own_copy(self):
        me = self.place.pipe
        return pltpu.make_async_copy(self.piece(me), self.spot(me, me), self.own_sem.at[0])

    def spread(self):
        me = self.place.pipe
        self.own_copy().start()
        for q in range(PHASES):
            @pl.when(q != me)
            def _():
                self.first(q, me, q).start()
                self.gain_copy(me, q).start()

            @pl.when(q == me)
            def _():
                self.gains[q] = self.gain[...]

    def arrived(self, s):
        @pl.when(s != self.place.pipe)
        def _():
            self.first(s, s, s).wait_recv()

        @pl.when(s == self.place.pipe)
        def _():
            self.own_copy().wait()

    def gains_arrived(self):
        for q in range(PHASES):
            @pl.when(q != self.place.pipe)
            def _():
                self.first(q, self.place.pipe, q).wait_send()
                self.gain_copy(self.place.pipe, q).wait_send()
                self.gain_copy(q, q).wait_recv()

    def copies(self, stage, s):
        place = self.place
        made = []

        def add(view, device):
            i = GATHER_BASE[stage] + len(made)
            made.append(pltpu.make_async_remote_copy(
                src_ref=view, dst_ref=view, send_sem=self.send.at[s, i], recv_sem=self.recv.at[s, i],
                device_id=device, device_id_type=MESH))

        if stage == 5:
            add(self.weights.at[s, :, :, :, place.core], place.sibling())
            return made
        for k, (a, b, c) in enumerate(ORDERS):
            def view(**where):
                return block(self.weights, (s,), k, place.core, **{**place.at, **where})

            if stage == 0:
                for delta in (1, -1, 2):
                    add(view(), place.neighbour(c, delta))
            elif stage == 1:
                for delta in (1, -1):
                    add(view(**{c: WHOLE}), place.neighbour(b, delta))
            elif stage == 2:
                for h, delta in enumerate((1, -1)):
                    add(view(**{b: place.step(b, -delta), c: half(h)}), place.neighbour(b, delta))
            elif stage == 3:
                for delta in (1, -1):
                    add(view(**{b: WHOLE, c: WHOLE}), place.neighbour(a, delta))
            else:
                for h, delta in enumerate((1, -1)):
                    add(view(**{a: place.step(a, -delta), b: half(h), c: WHOLE}), place.neighbour(a, delta))
        return made

    def tick(self, t):
        def move(stage, s):
            if stage:
                for copy in self.copies(stage - 1, s):
                    copy.wait()
            else:
                self.arrived(s)
            if stage < 6:
                for copy in self.copies(stage, s):
                    copy.start()

        for stage in reversed(range(7)):
            turn = t - GATHER_START[stage]
            if stage < GATHER_GROUPED:
                @pl.when((turn >= 0) & (turn < PHASES // GATHER_GROUP))
                def _():
                    def one(n, carry):
                        move(stage, turn * GATHER_GROUP + n)
                        return carry

                    lax.fori_loop(0, GATHER_GROUP, one, 0)
            else:
                @pl.when((turn >= 0) & (turn < PHASES))
                def _():
                    move(stage, turn)


STRIP = (3, 16, D // 4)
STAGE_BASE = (0, 1, 7, 13, 19, 25)
WIDE_PEERS = 16


def cut(ref, lead, k, where):
    index = []
    for axis in ORDERS[k]:
        if axis in where:
            v = where[axis]
            index.append(pl.ds(2 * v[1], 2) if isinstance(v, tuple) else v)
    return ref.at[(*lead, *index)]


def add_into(out, *parts):
    if len(parts) == 2:
        out[...] = parts[0][...] + parts[1][...]
        return
    total = parts[0][...].astype(F32)
    for part in parts[1:]:
        total += part[...].astype(F32)
    out[...] = total.astype(out.dtype)


SCATTER_START = (0, 1, 3, 5, 6, 7, 8)
WIDE_SLOTS = 4


class Scatter:
    def __init__(self, place, bufs):
        self.place = place
        (self.grad, self.pair, self.wide, self.wide_half, self.wide_got, self.slim, self.slim_half,
         self.slim_got, self.last, self.last_got, self.final, self.out, self.send, self.recv,
         self.final_send, self.final_recv) = bufs

    def copies(self, stage, i):
        place, slot, broad, sem = self.place, i % 2, i % WIDE_SLOTS, i % 4
        made = []

        def add(src, dst, device):
            j = STAGE_BASE[stage] + len(made)
            made.append(pltpu.make_async_remote_copy(
                src_ref=src, dst_ref=dst, send_sem=self.send.at[sem, j], recv_sem=self.recv.at[sem, j],
                device_id=device, device_id_type=MESH))

        if stage == 0:
            add(self.grad.at[:, :, :, 1 - place.core], self.pair.at[slot], place.sibling())
            return made
        for k, (a, b, c) in enumerate(ORDERS):
            if stage == 1:
                for h, delta in enumerate((1, -1)):
                    src = cut(self.wide, (broad, k), k, {a: place.step(a, 2), b: half(h)})
                    add(src, self.wide_half.at[broad, k, h], place.neighbour(a, delta))
            elif stage == 2:
                for h, delta in enumerate((1, -1)):
                    src = cut(self.wide, (broad, k), k, {a: place.step(a, delta)})
                    add(src, self.wide_got.at[broad, k, h], place.neighbour(a, delta))
            elif stage == 3:
                for h, delta in enumerate((1, -1)):
                    src = self.slim.at[slot, k, place.step(b, 2), pl.ds(2 * h, 2)]
                    add(src, self.slim_half.at[slot, k, h], place.neighbour(b, delta))
            elif stage == 4:
                for h, delta in enumerate((1, -1)):
                    src = self.slim.at[slot, k, place.step(b, delta)]
                    add(src, self.slim_got.at[slot, k, h], place.neighbour(b, delta))
            else:
                for h, delta in enumerate((1, -1, 2)):
                    src = self.last.at[slot, k, place.step(c, delta)]
                    add(src, self.last_got.at[slot, k, h], place.neighbour(c, delta))
        return made

    def fill_wide(self, i):
        slot, broad = i % 2, i % WIDE_SLOTS
        core = self.place.core

        def row(y, carry):
            for xh in range(2):
                for xl in range(2):
                    x = xh * 2 + xl
                    for k in range(3):
                        full = slice(None)
                        where = {"x": x, "y": y, "z": full}
                        out = self.wide.at[(broad, k, *(where[axis] for axis in ORDERS[k]))]
                        add_into(out, self.grad.at[y, xh, :, core, xl, k], self.pair.at[slot, y, xh, :, xl, k])
            return carry

        lax.fori_loop(0, 4, row, 0)

    def process(self, stage, i):
        place, slot, broad = self.place, i % 2, i % WIDE_SLOTS
        if stage == 1:
            self.fill_wide(i)
            return
        for k, (a, b, c) in enumerate(ORDERS):
            if stage == 2:
                for h, delta in enumerate((1, -1)):
                    part = self.wide.at[broad, k, place.step(a, delta), pl.ds(2 * h, 2)]
                    add_into(part, part, self.wide_half.at[broad, k, h])
            elif stage == 3:
                add_into(self.slim.at[slot, k], self.wide.at[broad, k, place.at[a]],
                         self.wide_got.at[broad, k, 0], self.wide_got.at[broad, k, 1])
            elif stage == 4:
                for h, delta in enumerate((1, -1)):
                    part = self.slim.at[slot, k, place.step(b, delta), pl.ds(2 * h, 2)]
                    add_into(part, part, self.slim_half.at[slot, k, h])
            elif stage == 5:
                add_into(self.last.at[slot, k], self.slim.at[slot, k, place.at[b]],
                         self.slim_got.at[slot, k, 0], self.slim_got.at[slot, k, 1])
            else:
                add_into(self.final.at[PHASES - 1 - i, k], self.last.at[slot, k, place.at[c]],
                         *(self.last_got.at[slot, k, h] for h in range(3)))

    def final_copy(self, s, source, target):
        return pltpu.make_async_remote_copy(
            src_ref=self.final.at[s], dst_ref=self.out.at[source],
            send_sem=self.final_send.at[s], recv_sem=self.final_recv.at[source],
            device_id=(target, self.place.dp), device_id_type=MESH)

    def deliver(self, i):
        me, s = self.place.pipe, PHASES - 1 - i

        @pl.when(s != me)
        def _():
            self.final_copy(s, me, s).start()

        @pl.when(s == me)
        def _():
            self.out[s] = self.final[s]

    def settle(self):
        for q in range(PHASES):
            @pl.when(q != self.place.pipe)
            def _():
                self.final_copy(q, q, q).wait()

    def tick(self, t):
        for stage in range(6, 0, -1):
            i = t - SCATTER_START[stage]

            @pl.when((i >= 0) & (i < PHASES))
            def _():
                for copy in self.copies(stage - 1, i):
                    copy.wait()
                self.process(stage, i)
                if stage < 6:
                    for copy in self.copies(stage, i):
                        copy.start()
                else:
                    self.deliver(i)

    def begin(self, i):
        for copy in self.copies(0, i):
            copy.start()


class GainSum:
    def __init__(self, place, dgains, bufs):
        self.place, self.dgains = place, dgains
        (self.rows, self.wide, self.sum, self.send, self.recv, self.wide_send, self.wide_recv) = bufs

    def narrow(self, owner, source, target):
        return pltpu.make_async_remote_copy(
            src_ref=self.dgains.at[owner], dst_ref=self.rows.at[source],
            send_sem=self.send.at[owner], recv_sem=self.recv.at[source],
            device_id=(target, self.place.dp), device_id_type=MESH)

    def share(self, index, source, target):
        return pltpu.make_async_remote_copy(
            src_ref=self.sum, dst_ref=self.wide.at[source],
            send_sem=self.wide_send.at[index], recv_sem=self.wide_recv.at[source],
            device_id=(self.place.pipe, target), device_id_type=MESH)

    def start(self):
        me = self.place.pipe
        for q in range(PHASES):
            @pl.when(q != me)
            def _():
                self.narrow(q, me, q).start()

            @pl.when(q == me)
            def _():
                self.rows[q] = self.dgains[q]

    def middle(self):
        for q in range(PHASES):
            @pl.when(q != self.place.pipe)
            def _():
                self.narrow(q, q, q).wait()
        self.sum[...] = jnp.sum(self.rows[...], axis=0)
        for q in range(WIDE_PEERS):
            @pl.when(q != self.place.dp)
            def _():
                self.share(q, self.place.dp, q).start()

            @pl.when(q == self.place.dp)
            def _():
                self.wide[q] = self.sum[...]

    def finish(self, total, swap):
        for q in range(WIDE_PEERS):
            @pl.when(q != self.place.dp)
            def _():
                self.share(q, q, q).wait()
        rows = jnp.sum(self.wide[...], axis=0)
        moved = dot(rows, swap.astype(F32), NN, lax.Precision.HIGHEST)
        total[0] = rows[0:2] + moved[2:4]


def head(j):
    return pl.ds(j * HEAD, HEAD)


def mix_phase(s, tabs, swap, hs, qs, ks, es, ms, ns, cols, mt):
    a0, b0, a1, b1 = tabs
    ones = jnp.ones((TOK, HEAD), BF16)
    for j in range(HEADS):
        hj = hs[s, :, head(j)]
        hf = hj.astype(F32)
        r = lax.rsqrt(jnp.mean(hf * hf, axis=-1, keepdims=True) + 1e-6)
        cols[s, :, j : j + 1] = r
        n = hf * r
        nsw = dot(hj, swap) * r
        ns[s, :, head(j)] = nsw.astype(BF16)
        qs[s, :, head(j)] = (n * a0 + nsw * b0).astype(BF16)
        ks[s, :, head(j)] = (n * a1 + nsw * b1).astype(BF16)
    for j in range(HEADS):
        scores = dot(qs[s, :, head(j)], ks[s, :, head(j)], NT)
        es[s, :, head(j)] = jnp.exp(scores).astype(BF16)
    for j in range(HEADS):
        both = dot(es[s, :, head(j)], jnp.concatenate([hs[s, :, head(j)], ones], axis=1))
        inv = 1.0 / both[:, HEAD:]
        cols[s, :, 16 + j : 17 + j] = inv[:, 0:1]
        mixed = (both[:, :HEAD] * inv).astype(BF16)
        ms[s, :, head(j)] = mixed
        mt[s, head(j), :] = mixed.T


def project_phase(s, w_ref, hs, ms):
    for c in range(4):
        cols = pl.ds(c * 384, 384)
        update = dot(ms[s], w_ref[s % 2, c].reshape(D, D // 4))
        hs[s + 1, :, cols] = (hs[s, :, cols].astype(F32) + update).astype(BF16)


def weight_phase(s, g, mt, grad_ref):
    for y in range(4):
        for t in range(4):
            part = dot(mt[s, pl.ds(t * 384, 384), :], g[:, pl.ds(y * 384, 384)]).astype(BF16)
            grad_ref[y, t // 2, pl.ds(t % 2 * 2, 2)] = part.reshape(2, 2, 2, *STRIP)


def input_phase(s, w_ref, tabs, swap, g, gm, dsc, cosine, sine, hs, qs, ks, es, ms, ns, cols, mt):
    a0, b0, a1, b1 = tabs
    for c in range(4):
        total = None
        for y in range(4):
            w = w_ref[s % 2, y, c // 2, pl.ds(c % 2 * 2, 2)].reshape(384, D // 4)
            part = dot(g[:, pl.ds(y * 384, 384)], w, NT)
            total = part if total is None else total + part
        gm[:, pl.ds(c * 384, 384)] = total.astype(BF16)
    for j in range(HEADS):
        gmf = gm[:, head(j)].astype(F32) * cols[s, :, 16 + j : 17 + j]
        gmb = gmf.astype(BF16)
        delta = jnp.sum(gmf * ms[s, :, head(j)].astype(F32), axis=-1, keepdims=True)
        ga = dot(gmb, hs[s, :, head(j)], NT)
        dsc[:, head(j)] = (es[s, :, head(j)].astype(F32) * (ga - delta)).astype(BF16)
        gm[:, head(j)] = gmb
    sums = [jnp.zeros((8, HEAD), F32)] * 4

    def folded(total, value):
        return total + jnp.sum(value.reshape(TOK // 8, 8, HEAD), axis=0)

    for j in range(HEADS):
        hj = hs[s, :, head(j)]
        r = cols[s, :, j : j + 1]
        ds = dsc[:, head(j)]
        dq = dot(ds, ks[s, :, head(j)])
        dk = dot(ds, qs[s, :, head(j)], TN)
        n = hj.astype(F32) * r
        nsw = ns[s, :, head(j)].astype(F32)
        c, sn = cosine[...], sine[...]
        nc, sc = n * c, nsw * sn
        sums = [folded(t, v) for t, v in zip(sums, (nc * dq, sc * dq, nc * dk, sc * dk))]
        crossed = (dq * b0 + dk * b1).astype(BF16)
        dn = dq * a0 + dk * a1 + dot(crossed, swap, NT)
        dh = r * (dn - n * jnp.mean(dn * n, axis=-1, keepdims=True))
        gv = dot(es[s, :, head(j)], gm[:, head(j)], TN)
        g[:, head(j)] = (g[:, head(j)].astype(F32) + (dh + gv)).astype(BF16)
    return [jnp.sum(t, axis=0, keepdims=True) for t in sums]


LIVE = 6


def window_kernel(shard_ref, gain_ref, clip_ref, pos_ref, cot_ref, freq_ref, swap_ref, sign_ref,
                  w_ref, out_ref, total_ref, *rest):
    rest = iter(rest)
    take = lambda count: [next(rest) for _ in range(count)]
    saved = take(8)
    g, gm, dsc, cosine, sine, own_gains, gains, dgains, wbuf = take(9)
    gather_sems = take(7)
    scatter_bufs = take(16)
    gain_bufs = take(7)
    in_sem, w_sem = take(2)
    grad = scatter_bufs[0]
    hs = saved[0]
    place = Place()
    live = place.pipe < LIVE
    slot = jnp.minimum(place.pipe, LIVE - 1)
    clip_in = pltpu.make_async_copy(clip_ref.at[slot // 3, slot % 3], hs.at[0], in_sem.at[0])
    cot_in = pltpu.make_async_copy(cot_ref.at[slot // 3, slot % 3], g, in_sem.at[1])
    clip_in.start()
    cot_in.start()
    own_gains[...] = jnp.concatenate([gain_ref[0].astype(F32), jnp.zeros((6, HEAD), F32)], axis=0)
    greet(place)
    gather = Gather(place, shard_ref, own_gains, w_ref, gains, gather_sems)
    scatter = Scatter(place, scatter_bufs)
    sums = GainSum(place, dgains, gain_bufs)
    scale = 1.0 / math.sqrt(HEAD)
    gather.spread()
    positions = pos_ref[:, slot % 3, slot // 3, :].astype(F32)
    padded = jnp.concatenate([positions, jnp.zeros((5, TOK), F32)], axis=0)
    angles = dot(padded, freq_ref[...], TN, lax.Precision.HIGHEST)
    cosine[...] = jnp.cos(angles)
    sine[...] = jnp.sin(angles) * sign_ref[...]

    @pl.when(jnp.logical_not(live))
    def _():
        grad[...] = jnp.zeros_like(grad)
        dgains[...] = jnp.zeros_like(dgains)

    clip_in.wait()
    cot_in.wait()

    def tables(s):
        rows = gains[s]
        moved = dot(rows.astype(BF16), swap_ref[...])
        c, n = cosine[...], sine[...]
        return (c * (rows[0:1] * scale), n * (moved[0:1] * scale), c * rows[1:2], n * moved[1:2])

    def weights_in(s):
        return pltpu.make_async_copy(w_ref.at[s], wbuf.at[s % 2], w_sem.at[s % 2])

    arrive = GATHER_START[6]

    def forward_tick(t, carry):
        gather.tick(t)
        ready = t - arrive

        @pl.when(ready >= 0)
        def _():
            weights_in(ready).start()

        @pl.when(t == arrive - 3)
        def _():
            gather.gains_arrived()

            @pl.when(live)
            def _():
                mix_phase(0, tables(0), swap_ref[...], *saved)

        @pl.when(ready >= 1)
        def _():
            s = ready - 1
            weights_in(s).wait()

            @pl.when(live)
            def _():
                project_phase(s, wbuf, hs, saved[4])
                mix_phase(s + 1, tables(s + 1), swap_ref[...], *saved)

        return carry

    lax.fori_loop(0, PHASES + arrive, forward_tick, 0)

    def backward_tick(t, carry):
        scatter.tick(t)

        @pl.when(t < PHASES)
        def _():
            s = PHASES - 1 - t

            @pl.when(live)
            def _():
                weight_phase(s, g, saved[7], grad)

            scatter.begin(t)

            @pl.when(t != 1)
            def _():
                weights_in(s).wait()

            @pl.when(live)
            def _():
                x0, y0, x1, y1 = input_phase(s, wbuf, tables(s), swap_ref[...], g, gm, dsc, cosine, sine, *saved)
                dgains[s] = jnp.concatenate([x0 * scale, x1, y0 * scale, y1, jnp.zeros((4, HEAD), F32)], axis=0)

            @pl.when(t < PHASES - 2)
            def _():
                weights_in(s - 2).start()

        @pl.when(t == PHASES)
        def _():
            sums.start()

        @pl.when(t == PHASES + 2)
        def _():
            sums.middle()

        return carry

    lax.fori_loop(0, PHASES + SCATTER_START[6], backward_tick, 0)
    sums.finish(total_ref, swap_ref[...])
    scatter.settle()
    for y in range(4):
        for xl in range(2):
            out_ref[xl, :, :, pl.ds(y * (D // 4), D // 4)] = scatter.out[y * 2 + xl].astype(F32)


def window(shard, gain_pair, clips, positions, cotangent):
    freq, swap, sign = rotary_constants()
    piece = (16, D // 4)
    sems = pltpu.SemaphoreType.DMA
    vmem = pl.BlockSpec(memory_space=pltpu.VMEM)
    anywhere = pl.BlockSpec(memory_space=pl.ANY)
    rows = pltpu.VMEM((PHASES, TOK, D), BF16)
    columns = pltpu.VMEM((PHASES, TOK, HEAD), F32)
    scratch = [
        rows, rows, rows, rows, rows, rows, columns, pltpu.VMEM((PHASES, D, TOK), BF16),
        pltpu.VMEM((TOK, D), BF16),
        pltpu.VMEM((TOK, D), BF16),
        pltpu.VMEM((TOK, D), BF16),
        pltpu.VMEM((TOK, HEAD), F32),
        pltpu.VMEM((TOK, HEAD), F32),
        pltpu.VMEM((8, HEAD), F32),
        pltpu.VMEM((PHASES, 8, HEAD), F32),
        pltpu.VMEM((PHASES, 8, HEAD), F32),
        pltpu.VMEM((2, *TILES), BF16),
        sems((PHASES,)), sems((PHASES,)), sems((PHASES,)), sems((PHASES,)), sems((1,)),
        sems((PHASES, 34)), sems((PHASES, 34)),
        pltpu.VMEM(TILES, BF16),
        pltpu.VMEM((2, 4, 2, 4, 2, *STRIP), BF16),
        pltpu.VMEM((WIDE_SLOTS, 3, 4, 4, 4, *piece), BF16),
        pltpu.VMEM((WIDE_SLOTS, 3, 2, 2, 4, *piece), BF16),
        pltpu.VMEM((WIDE_SLOTS, 3, 2, 4, 4, *piece), BF16),
        pltpu.VMEM((2, 3, 4, 4, *piece), BF16),
        pltpu.VMEM((2, 3, 2, 2, *piece), BF16),
        pltpu.VMEM((2, 3, 2, 4, *piece), BF16),
        pltpu.VMEM((2, 3, 4, *piece), BF16),
        pltpu.VMEM((2, 3, 3, *piece), BF16),
        pltpu.VMEM((PHASES, *STRIP), BF16),
        pltpu.VMEM((PHASES, *STRIP), BF16),
        sems((4, 34)), sems((4, 34)), sems((PHASES,)), sems((PHASES,)),
        pltpu.VMEM((PHASES, 8, HEAD), F32),
        pltpu.VMEM((WIDE_PEERS, 8, HEAD), F32),
        pltpu.VMEM((8, HEAD), F32),
        sems((PHASES,)), sems((PHASES,)), sems((WIDE_PEERS,)), sems((WIDE_PEERS,)),
        sems((2,)), sems((2,)),
    ]
    return pl.pallas_call(
        window_kernel,
        out_shape=(
            jax.ShapeDtypeStruct((PHASES, *TILES), BF16),
            jax.ShapeDtypeStruct((2, 3, 16, D), F32),
            jax.ShapeDtypeStruct((1, 2, HEAD), F32),
        ),
        in_specs=[vmem, vmem, anywhere, vmem, anywhere, vmem, vmem, vmem],
        out_specs=[anywhere, vmem, vmem],
        scratch_shapes=scratch,
        compiler_params=pltpu.CompilerParams(
            collective_id=0, has_side_effects=True, vmem_limit_bytes=67_043_328
        ),
        name="window",
    )(
        shard, gain_pair, clips, positions.transpose(0, 2, 1, 3), cotangent, jnp.asarray(freq),
        jnp.asarray(swap, BF16), jnp.asarray(sign),
    )


def shards(clips, positions, out_proj, qk_gains, cotangent):
    _, shard, dgain = window(out_proj.reshape(1, 2, 3, 16, D), qk_gains, clips, positions, cotangent)
    return (shard.reshape(1, D // 16, D), dgain)


def solution(mesh):
    placed = (
        P(None, None, "dp", None),
        P(None, None, None, "dp"),
        P("pipe", "dp", None),
        P("pipe", None, None),
        P(None, None, "dp", None),
    )
    return jax.shard_map(
        shards,
        mesh=mesh,
        in_specs=placed,
        out_specs=(P("pipe", "dp", None), P("pipe", None, None)),
        check_vma=False,
    )
```
